256 devices in a mesh: grp: 8 (over z), tp: 32 (over x, y, core).
Axes of the slice: x: 4, y: 4, z: 8, core: 2. Of those that a mesh axis runs over, the one named last changes fastest.
Arguments:
- hidden: bfloat16 [8192, 20480], P('grp', 'tp'), may hold values from -6 to 6
- down_weight: bfloat16 [20480, 8192], P('tp'), may hold values from -0.078125 to 0.078125
- adapter_down_factor: bfloat16 [64, 64, 20480], P('grp', None, 'tp'), may hold values from -0.0390625 to 0.0390625
- adapter_up_factor: bfloat16 [64, 64, 8192], P('grp', None, 'tp'), may hold values from -0.75 to 0.75
- row_tile_adapter: int32 [64], P('grp'), may hold values from 0 to 63, as said below
- adapter_pool_slot: int32 [64], replicated, may hold values from 0 to 63, as said below
Outputs:
- output: bfloat16 [8192, 8192], P('grp', 'tp')
The draws below stay inside these ranges and needn't reach their ends.
Inputs may be any that keep to these rules, and one draw needn't show every extreme that they name: adapter_pool_slot is a permutation; slot s of the pool is held by group s // 8. `row_tile_adapter`: at most 4 tiles of one group have adapters held by one owner group, and in every draw one owner group holds the adapters of exactly 4 tiles of every group.
All inputs are finite; a program needn't handle non-finite values.
Results may differ from the reference program's by a relative error of at most 0.019.
Values may be sent and summed in bfloat16 or wider, within the bound.
A program may use at most 128 MiB of HBM per device.

```python
import jax
import jax.numpy as jnp
from jax import lax

MODEL_WIDTH = 8192
HIDDEN_SPAN = 20480
ADAPTER_RANK = 64
TILE = 128
TILES_GRP = 8
ADP_GRP = 8
TOKENS = 8192
TILES = 64
ADAPTER_POOL = 64
N_TP = 32


def routing_tables(key):
    group_count = TILES // TILES_GRP
    adapter_slot = jax.random.permutation(jax.random.fold_in(key, 11), ADAPTER_POOL).astype(jnp.int32)
    slot_adapter = jnp.argsort(adapter_slot).astype(jnp.int32)
    hot_owner = jax.random.randint(jax.random.fold_in(key, 12), (), 0, group_count)
    half_count = TILES_GRP // 2
    others = (hot_owner + 1 + jax.random.randint(jax.random.fold_in(key, 13), (group_count, half_count), 0, group_count - 1)) % group_count
    owners = jnp.concatenate([jnp.full((group_count, half_count), hot_owner, jnp.int32), others.astype(jnp.int32)], axis=1)
    scores = jax.random.randint(jax.random.fold_in(key, 14), (group_count, TILES_GRP), 0, 1 << 20) * TILES_GRP + jnp.arange(TILES_GRP, dtype=jnp.int32)[None, :]
    shuffle = jnp.argsort(scores, axis=1)
    owners = jnp.take_along_axis(owners, shuffle, axis=1)
    picked = jax.random.randint(jax.random.fold_in(key, 15), (group_count, TILES_GRP), 0, ADP_GRP)
    tile_table = slot_adapter[owners * ADP_GRP + picked].reshape(group_count * TILES_GRP).astype(jnp.int32)
    return (adapter_slot, tile_table)


def draw_row_tile_adapter(key, part):
    return routing_tables(key)[1]


def draw_adapter_pool_slot(key, part):
    return routing_tables(key)[0]


def spiked(result, own_key, source, target, shards_of, factor):
    def block_of(axis_at):
        return (jnp.arange(result.shape[axis_at]) // (result.shape[axis_at] // shards_of)).reshape((-1,) + (1,) * (result.ndim - 1 - axis_at))

    one_side = jax.random.permutation(own_key, shards_of)[block_of(target)]
    far = (block_of(target) + shards_of // 2) % shards_of
    return jnp.where((block_of(source) == one_side) | (block_of(source) == far), factor * result, result)


def block_levels(own_key, shape, split, low, largest):
    def one(axis_at, blocks):
        heights = jax.random.uniform(jax.random.fold_in(jax.random.fold_in(own_key, 6), axis_at), (blocks,), jnp.float32, low / len(split), largest / len(split))
        return jnp.repeat(jnp.exp(heights), shape[axis_at] // blocks).reshape((-1,) + (1,) * (len(shape) - axis_at - 1))

    factor_of = one(*split[0])
    for cut in split[1:]:
        factor_of = factor_of * one(*cut)
    return factor_of


def bell_draw(rng, dims, deviation, bound, cuts=(), held_as=jnp.bfloat16):
    factor_of = block_levels(rng, dims, cuts, -0.22, 0.18) if cuts else 1.0
    result = jax.random.normal(rng, dims, jnp.float32) * deviation * factor_of
    return jnp.minimum(jnp.maximum(result, -bound), bound).astype(held_as)


def bell_draw_with(own_key, dims, deviation, bound, pieces, heavy, kind=jnp.bfloat16):
    entries = deviation * jax.random.normal(own_key, dims, jnp.float32)
    if pieces:
        entries = entries * block_levels(own_key, dims, pieces, -0.22, 0.18)
    return jnp.clip(spiked(entries, jax.random.fold_in(own_key, 3), *heavy), -bound, bound).astype(kind)


def setup_inputs(seed: int = 0) -> dict:
    key_list = jax.random.split(jax.random.key(seed), 7)
    hidden = bell_draw(key_list[0], (TOKENS, HIDDEN_SPAN), 1.0, 6.0, ((0, 8), (1, 32)))
    down_weight = bell_draw_with(key_list[1], (HIDDEN_SPAN, MODEL_WIDTH), HIDDEN_SPAN ** -0.5, 0.078125, ((0, 32),), (0, 1, 32, 2.75))
    adapter_down_factor = bell_draw(key_list[2], (ADAPTER_POOL, ADAPTER_RANK, HIDDEN_SPAN), HIDDEN_SPAN ** -0.5, 0.0390625, ((0, 8), (2, 32)))
    adapter_up_factor = bell_draw(key_list[3], (ADAPTER_POOL, ADAPTER_RANK, MODEL_WIDTH), ADAPTER_RANK ** -0.5, 0.75, ((0, 8), (2, 32)))
    row_tile_adapter = draw_row_tile_adapter(jax.random.fold_in(key_list[6], 71), 0)
    adapter_pool_slot = draw_adapter_pool_slot(jax.random.fold_in(key_list[6], 71), 0)
    return {"hidden": hidden, "down_weight": down_weight, "adapter_down_factor": adapter_down_factor, "adapter_up_factor": adapter_up_factor, "row_tile_adapter": row_tile_adapter, "adapter_pool_slot": adapter_pool_slot}


adapter_scale = 2.0


def reference(hidden, down_weight, adapter_down_factor, adapter_up_factor, row_tile_adapter, adapter_pool_slot):
    block_width = HIDDEN_SPAN // N_TP

    def accumulate(running, block_index):
        offset_cols = (block_index * block_width).astype(jnp.int32)
        hidden_block = lax.dynamic_slice_in_dim(hidden, offset_cols, block_width, 1)
        weight_rows = lax.dynamic_slice_in_dim(down_weight, offset_cols, block_width, 0)
        partial_value = jnp.dot(hidden_block, weight_rows, preferred_element_type=jnp.float32).astype(jnp.bfloat16)
        return running + partial_value.astype(jnp.float32), None

    base, _ = lax.scan(accumulate, jnp.zeros((TOKENS, MODEL_WIDTH), jnp.float32), jnp.arange(N_TP, dtype=jnp.int32))
    slot_table = adapter_pool_slot[row_tile_adapter].astype(jnp.int32)
    tile_rows = hidden.reshape(TILES, TILE, HIDDEN_SPAN).astype(jnp.float32)
    selected_down = adapter_down_factor[slot_table].astype(jnp.float32)
    rank_projections = jnp.einsum("ktf,krf->ktr", tile_rows, selected_down).astype(jnp.bfloat16)
    selected_up = adapter_up_factor[slot_table].astype(jnp.float32)
    adapted_output = (jnp.einsum("pjf,pfb->pjb", rank_projections.astype(jnp.float32), selected_up) * adapter_scale).astype(jnp.bfloat16)
    return (base + adapted_output.reshape(TOKENS, MODEL_WIDTH).astype(jnp.float32)).astype(jnp.bfloat16)
```

```python
import jax
import jax.numpy as jnp
from jax import lax
from jax.experimental import pallas as pl
from jax.experimental.pallas import tpu as pltpu
from jax.sharding import PartitionSpec as P

adapter_scale = 2.0
MESH = pl.DeviceIdType.MESH
NX, NY, NZ, NTP = 4, 4, 8, 32
BF, F32 = jnp.bfloat16, jnp.float32
BLOCK_ORDER = (
    (2, 2), (2, 1), (1, 2), (2, 3), (3, 2), (2, 0), (0, 2), (1, 1),
    (1, 3), (3, 1), (3, 3), (1, 0), (3, 0), (0, 1), (0, 3), (0, 0),
)


def kernel(
    hid, wgt, down, up, tiles, slots, out,
    h_own, h_sib, w_own, w_sib, send1, recv1, send2, recv2, part, hold,
    p_down, s_down, a_down, p_up, s_up, a_up, slot_out, slot_in, slot_s,
    rank_out, rank_in, rank_sum, rank_all,
    l_sem, hs_s, hs_r, ws_s, ws_r, s1_s, s1_r, s2_s, s2_r,
    zs_s, zs_r, zd1_s, zd1_r, zu1_s, zu1_r, zd2_s, zd2_r, zu2_s, zu2_r,
    ra_s, ra_r, rb_s, rb_r, loc_sem,
):
    z = lax.axis_index("grp")
    t = lax.axis_index("tp")
    core = lax.rem(t, 2)
    y = lax.rem(t // 2, NY)
    x = t // (2 * NY)

    def at(xx, yy, cc):
        return {"grp": z, "tp": (lax.rem(xx, NX) * NY + lax.rem(yy, NY)) * 2 + cc}

    def at_z(zz):
        return {"grp": zz, "tp": t}

    def at_t(tt):
        return {"grp": z, "tp": tt}

    def remote(src, dst, ssem, rsem, dev):
        return pltpu.make_async_remote_copy(
            src_ref=src, dst_ref=dst, send_sem=ssem, recv_sem=rsem,
            device_id=dev, device_id_type=MESH,
        )

    sib = at(x, y, 1 - core)

    def load_h(q):
        r = pl.ds(q * 256, 256)
        return pltpu.make_async_copy(hid.at[r], h_own.at[r], l_sem.at[q])

    def blk(ox, oy):
        return lax.rem(x + ox, NX) * NY + lax.rem(y + oy, NY)

    def load_w(b):
        c = pl.multiple_of((2 * b + core) * 256, 256)
        return pltpu.make_async_copy(wgt.at[:, pl.ds(c, 256)], w_own.at[b], l_sem.at[4 + b])

    def swap_h(q):
        r = pl.ds(q * 256, 256)
        return remote(hid.at[r], h_sib.at[r], hs_s.at[q], hs_r.at[q], sib)

    def swap_w(b):
        c = pl.multiple_of((2 * b + 1 - core) * 256, 256)
        return remote(wgt.at[:, pl.ds(c, 256)], w_sib.at[b], ws_s.at[b], ws_r.at[b], sib)

    for q in range(4):
        load_h(q).start()
    for ox, oy in BLOCK_ORDER:
        load_w(blk(ox, oy)).start()
    own_down = pltpu.make_async_copy(down.at[:, z], p_down.at[pl.ds(z * 8, 8)], loc_sem.at[0])
    own_up = pltpu.make_async_copy(up.at[:, z], p_up.at[pl.ds(z * 8, 8)], loc_sem.at[1])
    own_down.start()
    own_up.start()

    row = lax.broadcasted_iota(jnp.int32, (8, 128), 0)
    mine = jnp.zeros((8, 128), jnp.int32)
    for i in range(8):
        mine = jnp.where(row == i, slots[tiles[i]], mine)
    slot_out[...] = mine

    barrier = pltpu.get_barrier_semaphore()

    def greet_t(i, _):
        pl.semaphore_signal(barrier, inc=1, device_id=at_t(lax.rem(t + i, NTP)), device_id_type=MESH)
        return 0

    def greet_z(i, _):
        pl.semaphore_signal(barrier, inc=1, device_id=at_z(lax.rem(z + i, NZ)), device_id_type=MESH)
        return 0

    lax.fori_loop(1, NZ, greet_z, 0)
    lax.fori_loop(1, NTP, greet_t, 0)
    pl.semaphore_wait(barrier, NTP - 1 + NZ - 1)

    def z_slot(p):
        return remote(slot_out, slot_in.at[z], zs_s.at[p], zs_r.at[z], at_z(p))

    def z_down1(p):
        return remote(down.at[:, p], p_down.at[pl.ds(z * 8, 8)], zd1_s.at[p], zd1_r.at[z], at_z(p))

    def z_up1(p):
        return remote(up.at[:, p], p_up.at[pl.ds(z * 8, 8)], zu1_s.at[p], zu1_r.at[z], at_z(p))

    def z_down2(p):
        return remote(s_down.at[p], a_down.at[:, z], zd2_s.at[p], zd2_r.at[z], at_z(p))

    def z_up2(p):
        return remote(s_up.at[p], a_up.at[:, z], zu2_s.at[p], zu2_r.at[z], at_z(p))

    def each_z(make):
        def body(i, _):
            make(lax.rem(z + i, NZ))
            return 0
        lax.fori_loop(1, NZ, body, 0)

    def got(dst, sem):
        pltpu.make_async_copy(dst, dst, sem).wait()

    for q in range(4):
        swap_h(q).start()
    swap_w(blk(2, 2)).start()
    each_z(lambda p: z_slot(p).start())
    each_z(lambda p: z_down1(p).start())
    for ox, oy in BLOCK_ORDER[1:]:
        swap_w(blk(ox, oy)).start()
    each_z(lambda p: z_up1(p).start())

    def product(q, b):
        r = pl.ds(pl.multiple_of(q * 256, 256), 256)
        return jnp.dot(h_own[r, :], w_own[b], preferred_element_type=F32) + jnp.dot(
            h_sib[r, :], w_sib[b], preferred_element_type=F32
        )

    def order(j):
        return jnp.where(j == 0, 2, jnp.where(j == 1, 1, jnp.where(j == 2, 3, 0)))

    def block_of(f, along, across):
        first = f // 2 == 0
        return blk(jnp.where(first, along, across), jnp.where(first, across, along))

    def ahead(f):
        return jnp.where(lax.rem(f, 2) == 0, 1, 3)

    def other(f):
        return f + 1 - 2 * lax.rem(f, 2)

    def peer1(f):
        first = f // 2 == 0
        d = ahead(f)
        return at(x + jnp.where(first, d, 0), y + jnp.where(first, 0, d), core)

    def peer2(f):
        first = f // 2 == 0
        d = ahead(f)
        return at(x + jnp.where(first, 0, d), y + jnp.where(first, d, 0), core)

    def copy1(f, s, j):
        return remote(send1.at[f, s, j], recv1.at[f, s, j], s1_s.at[f, s, j], s1_r.at[f, s, j], peer1(f))

    def copy2(f, s):
        return remote(send2.at[f, s], recv2.at[f, s], s2_s.at[f, s], s2_r.at[f, s], peer2(f))

    for q in range(4):
        load_h(q).wait()
        swap_h(q).wait_recv()

    def need_w(b):
        load_w(b).wait()
        swap_w(b).wait_recv()

    def step0(i, _):
        j = i // 4
        f = lax.rem(i, 4)
        o = order(j)

        @pl.when(f == 0)
        def _():
            need_w(blk(2, o))

        @pl.when((f == 2) & (j > 0))
        def _():
            need_w(blk(o, 2))

        send1[f, 0, j] = product(f, block_of(f, 2, o)).astype(BF)
        copy1(f, 0, j).start()
        return 0

    lax.fori_loop(0, 16, step0, 0)
    for ox, oy in BLOCK_ORDER[7:]:
        need_w(blk(ox, oy))

    def step1(i, _):
        j = i // 4
        f = lax.rem(i, 4)
        send1[f, 1, j] = product(other(f), block_of(f, ahead(f), order(j))).astype(BF)
        copy1(f, 1, j).start()
        return 0

    lax.fori_loop(0, 16, step1, 0)

    def step2(i, _):
        j = i // 4
        f = lax.rem(i, 4)
        v = product(f, block_of(f, ahead(f), order(j)))
        copy1(f, 0, j).wait_recv()
        send1[f, 2, j] = (v + recv1[f, 0, j].astype(F32)).astype(BF)
        copy1(f, 2, j).start()
        return 0

    lax.fori_loop(0, 16, step2, 0)

    def take_slots(p):
        got(slot_in.at[p], zs_r.at[p])
        cp = pltpu.make_async_copy(slot_in.at[p], slot_s.at[p], loc_sem.at[2])
        cp.start()
        cp.wait()

    each_z(take_slots)
    cp = pltpu.make_async_copy(slot_out, slot_s.at[z], loc_sem.at[2])
    cp.start()
    cp.wait()

    own_down.wait()
    each_z(lambda p: got(p_down.at[pl.ds(p * 8, 8)], zd1_r.at[p]))

    def choose(src, dst):
        def body_for(p):
            def body(i, _):
                dst[p, i] = src[slot_s[p, i, 0]]
                return 0
            lax.fori_loop(0, 8, body, 0)
        return body_for

    def send_down(p):
        choose(p_down, s_down)(p)
        z_down2(p).start()

    each_z(send_down)

    def keep_down(i, _):
        a_down[i, z] = p_down[slot_s[z, i, 0]]
        a_up[i, z] = p_up[slot_s[z, i, 0]]
        return 0

    def step3(i, _):
        j = i // 4
        f = lax.rem(i, 4)
        part[f, j] = product(f, block_of(f, 0, order(j)))
        return 0

    lax.fori_loop(0, 16, step3, 0)

    own_up.wait()
    each_z(lambda p: got(p_up.at[pl.ds(p * 8, 8)], zu1_r.at[p]))

    def send_up(p):
        choose(p_up, s_up)(p)
        z_up2(p).start()

    each_z(send_up)
    lax.fori_loop(0, 8, keep_down, 0)

    def total1(q, j):
        copy1(q, 2, j).wait_recv()
        copy1(other(q), 1, j).wait_recv()
        return part[q, j] + recv1[q, 2, j].astype(F32) + recv1[other(q), 1, j].astype(F32)

    def turn0(q, _):
        send2[q, 0] = total1(q, 0).astype(BF)
        copy2(q, 0).start()
        return 0

    lax.fori_loop(0, 4, turn0, 0)

    def turn1(i, _):
        j = 1 + i // 4
        q = lax.rem(i, 4)
        v = total1(q, j)
        keep = lax.rem(q, 2) == j - 1

        @pl.when(keep)
        def _():
            hold[q] = v

        @pl.when(jnp.logical_not(keep))
        def _():
            send2[other(q), 1] = v.astype(BF)
            copy2(other(q), 1).start()

        return 0

    lax.fori_loop(0, 8, turn1, 0)

    def turn2(q, _):
        v = hold[q]
        copy2(q, 0).wait_recv()
        send2[q, 2] = (v + recv2[q, 0].astype(F32)).astype(BF)
        copy2(q, 2).start()
        return 0

    lax.fori_loop(0, 4, turn2, 0)

    def turn3(q, _):
        part[q, 3] = total1(q, 3)
        return 0

    lax.fori_loop(0, 4, turn3, 0)

    each_z(lambda p: got(a_down.at[:, p], zd2_r.at[p]))

    def rank(i, _):
        r = pl.ds(pl.multiple_of(i * 128, 128), 128)
        v = lax.dot_general(
            a_down[i].reshape(64, 640), h_own[r, :], (((1,), (1,)), ((), ())),
            preferred_element_type=F32,
        )
        rank_out[pl.ds(i * 4, 4)] = v.astype(BF).reshape(4, 16, 128)
        return 0

    lax.fori_loop(0, 8, rank, 0)

    def copy_a(p):
        return remote(rank_out.at[p], rank_in.at[t], ra_s.at[p], ra_r.at[t], at_t(p))

    def copy_b(p):
        return remote(rank_sum, rank_all.at[t], rb_s.at[p], rb_r.at[t], at_t(p))

    def each_t(make):
        def body(i, _):
            make(lax.rem(t + i, NTP))
            return 0
        lax.fori_loop(1, NTP, body, 0)

    each_t(lambda p: copy_a(p).start())
    each_t(lambda p: got(rank_in.at[p], ra_r.at[p]))

    def add_rank(i, acc):
        return acc + rank_in[lax.rem(t + i, NTP)].astype(F32)

    total = lax.fori_loop(1, NTP, add_rank, rank_out[t].astype(F32)).astype(BF)
    rank_sum[...] = total
    rank_all[t] = total
    each_t(lambda p: copy_b(p).start())
    each_z(lambda p: got(a_up.at[:, p], zu2_r.at[p]))
    each_t(lambda p: got(rank_all.at[p], rb_r.at[p]))

    def finish(q, _):
        copy2(q, 2).wait_recv()
        copy2(other(q), 1).wait_recv()
        base = part[q, 3] + recv2[q, 2].astype(F32) + recv2[other(q), 1].astype(F32)
        for k in range(2):
            i = q * 2 + k
            v = lax.dot_general(
                rank_all[pl.ds(i * 4, 4)].reshape(64, 128), a_up[i].reshape(64, 256),
                (((0,), (0,)), ((), ())), preferred_element_type=F32,
            )
            delta = (v * adapter_scale).astype(BF).astype(F32)
            r = pl.ds(pl.multiple_of(i * 128, 128), 128)
            out[r, :] = (base[k * 128:(k + 1) * 128] + delta).astype(BF)
        return 0

    lax.fori_loop(0, 4, finish, 0)

    for q in range(4):
        swap_h(q).wait_send()

    def sent_w(b, _):
        swap_w(b).wait_send()
        return 0

    lax.fori_loop(0, 16, sent_w, 0)

    def sent1(i, _):
        f = i // 12
        s = lax.rem(i // 4, 3)
        copy1(f, s, lax.rem(i, 4)).wait_send()
        return 0

    lax.fori_loop(0, 48, sent1, 0)

    def sent2(i, _):
        copy2(i // 3, lax.rem(i, 3)).wait_send()
        return 0

    lax.fori_loop(0, 12, sent2, 0)

    def sent_z(p):
        z_slot(p).wait_send()
        z_down1(p).wait_send()
        z_up1(p).wait_send()
        z_down2(p).wait_send()
        z_up2(p).wait_send()

    each_z(sent_z)

    def sent_t(p):
        copy_a(p).wait_send()
        copy_b(p).wait_send()

    each_t(sent_t)


def local(hidden, down_weight, adapter_down_factor, adapter_up_factor, row_tile_adapter, adapter_pool_slot):
    any_ = pl.BlockSpec(memory_space=pl.ANY)
    smem = pl.BlockSpec(memory_space=pltpu.SMEM)
    V, D = pltpu.VMEM, pltpu.SemaphoreType.DMA
    down = adapter_down_factor.reshape(8, 8, 8, 640)
    up = adapter_up_factor.reshape(8, 8, 8, 256)
    return pl.pallas_call(
        kernel,
        out_shape=jax.ShapeDtypeStruct((1024, 256), BF),
        in_specs=[any_, any_, any_, any_, smem, smem],
        out_specs=pl.BlockSpec(memory_space=pltpu.VMEM),
        scratch_shapes=[
            V((1024, 640), BF), V((1024, 640), BF),
            V((16, 640, 256), BF), V((16, 640, 256), BF),
            V((4, 3, 4, 256, 256), BF), V((4, 3, 4, 256, 256), BF),
            V((4, 3, 256, 256), BF), V((4, 3, 256, 256), BF),
            V((4, 4, 256, 256), F32), V((4, 256, 256), F32),
            V((64, 8, 640), BF), V((8, 8, 8, 640), BF), V((8, 8, 8, 640), BF),
            V((64, 8, 256), BF), V((8, 8, 8, 256), BF), V((8, 8, 8, 256), BF),
            V((8, 128), jnp.int32), V((8, 8, 128), jnp.int32), pltpu.SMEM((8, 8, 128), jnp.int32),
            V((32, 16, 128), BF), V((32, 16, 128), BF), V((16, 128), BF), V((32, 16, 128), BF),
            D((20,)), D((4,)), D((4,)), D((16,)), D((16,)),
            D((4, 3, 4)), D((4, 3, 4)), D((4, 3)), D((4, 3)),
            D((8,)), D((8,)), D((8,)), D((8,)), D((8,)), D((8,)),
            D((8,)), D((8,)), D((8,)), D((8,)),
            D((32,)), D((32,)), D((32,)), D((32,)), D((3,)),
        ],
        compiler_params=pltpu.CompilerParams(
            collective_id=0, has_side_effects=True, vmem_limit_bytes=60 * 2**20
        ),
    )(hidden, down_weight, down, up, row_tile_adapter, adapter_pool_slot)


def solution(mesh):
    placed = (
        P("grp", "tp"), P("tp", None), P("grp", None, "tp"), P("grp", None, "tp"), P("grp"), P(),
    )
    return jax.shard_map(local, mesh=mesh, in_specs=placed, out_specs=P("grp", "tp"), check_vma=False)
```

```python
import jax
import jax.numpy as jnp
from jax import lax
from jax.experimental import pallas as pl
from jax.experimental.pallas import tpu as pltpu
from jax.sharding import PartitionSpec as P

adapter_scale = 2.0
MESH = pl.DeviceIdType.MESH
NX, NY, NZ, NTP = 4, 4, 8, 32
BF, F32 = jnp.bfloat16, jnp.float32
DEPTH = 4
BLOCK_ORDER = (
    (2, 2), (2, 1), (1, 2), (2, 3), (3, 2), (2, 0), (0, 2), (1, 1),
    (1, 3), (3, 1), (3, 3), (1, 0), (3, 0), (0, 1), (0, 3), (0, 0),
)


def kernel(
    hid, wgt, down, up, tiles, slots, out,
    h_own, h_sib, w_own, w_sib, send1, recv1, send2, recv2, part, hold,
    p_down, s_down, a_down, p_up, s_up, a_up, slot_out, slot_in, slot_s,
    rank_out, rank_in, rank_sum, rank_all,
    l_sem, hs_s, hs_r, ws_s, ws_r, s1_s, s1_r, s2_s, s2_r,
    zs_s, zs_r, zd1_s, zd1_r, zu1_s, zu1_r, zd2_s, zd2_r, zu2_s, zu2_r,
    ra_s, ra_r, rb_s, rb_r, loc_sem, slot_sem, ready_p, ready_z,
):
    z = lax.axis_index("grp")
    t = lax.axis_index("tp")
    core = lax.rem(t, 2)
    y = lax.rem(t // 2, NY)
    x = t // (2 * NY)

    def at(xx, yy, cc):
        return {"grp": z, "tp": (lax.rem(xx, NX) * NY + lax.rem(yy, NY)) * 2 + cc}

    def at_z(zz):
        return {"grp": zz, "tp": t}

    def at_t(tt):
        return {"grp": z, "tp": tt}

    def remote(src, dst, ssem, rsem, dev):
        return pltpu.make_async_remote_copy(
            src_ref=src, dst_ref=dst, send_sem=ssem, recv_sem=rsem,
            device_id=dev, device_id_type=MESH,
        )

    sib = at(x, y, 1 - core)

    def load_h(q):
        r = pl.ds(q * 256, 256)
        return pltpu.make_async_copy(hid.at[r], h_own.at[r], l_sem.at[q])

    def blk(ox, oy):
        return lax.rem(x + ox, NX) * NY + lax.rem(y + oy, NY)

    def load_w(b):
        c = pl.multiple_of((2 * b + core) * 256, 256)
        return pltpu.make_async_copy(wgt.at[:, pl.ds(c, 256)], w_own.at[b], l_sem.at[4 + b])

    def swap_h(q):
        r = pl.ds(q * 256, 256)
        return remote(hid.at[r], h_sib.at[r], hs_s.at[q], hs_r.at[q], sib)

    def swap_w(b):
        c = pl.multiple_of((2 * b + 1 - core) * 256, 256)
        return remote(wgt.at[:, pl.ds(c, 256)], w_sib.at[b], ws_s.at[b], ws_r.at[b], sib)

    for q in range(4):
        load_h(q).start()
    for ox, oy in BLOCK_ORDER:
        load_w(blk(ox, oy)).start()
    own_down = pltpu.make_async_copy(down.at[:, z], p_down.at[pl.ds(z * 8, 8)], loc_sem.at[0])
    own_up = pltpu.make_async_copy(up.at[:, z], p_up.at[pl.ds(z * 8, 8)], loc_sem.at[1])
    own_down.start()
    own_up.start()

    row = lax.broadcasted_iota(jnp.int32, (8, 128), 0)
    mine = jnp.zeros((8, 128), jnp.int32)
    for i in range(8):
        mine = jnp.where(row == i, slots[tiles[i]], mine)
    slot_out[...] = mine

    barrier = pltpu.get_barrier_semaphore()

    near_plane = [sib] + [at(x + d, y, core) for d in (1, 3)] + [at(x, y + d, core) for d in (1, 3)]
    near_z = [at_z(lax.rem(z + d, NZ)) for d in (1, NZ - 1)]

    def tell(sem, devices):
        for dev in devices:
            pl.semaphore_signal(sem, inc=1, device_id=dev, device_id_type=MESH)

    tell(barrier, near_plane + near_z)
    pl.semaphore_wait(barrier, 7)

    def hear_plane(k):
        pl.semaphore_wait(ready_p.at[k], 5)

    def hear_z(k):
        pl.semaphore_wait(ready_z.at[k], 2)

    tell(ready_z.at[0], near_z)
    tell(ready_p.at[0], near_plane)

    def z_slot(p):
        return remote(slot_out, slot_in.at[z], zs_s.at[p], zs_r.at[z], at_z(p))

    def z_down1(p):
        return remote(down.at[:, p], p_down.at[pl.ds(z * 8, 8)], zd1_s.at[p], zd1_r.at[z], at_z(p))

    def z_up1(p):
        return remote(up.at[:, p], p_up.at[pl.ds(z * 8, 8)], zu1_s.at[p], zu1_r.at[z], at_z(p))

    def z_down2(p):
        return remote(s_down.at[p], a_down.at[:, z], zd2_s.at[p], zd2_r.at[z], at_z(p))

    def z_up2(p):
        return remote(s_up.at[p], a_up.at[:, z], zu2_s.at[p], zu2_r.at[z], at_z(p))

    def each_z(make):
        def body(i, _):
            make(lax.rem(z + i, NZ))
            return 0
        lax.fori_loop(1, NZ, body, 0)

    def got(dst, sem):
        pltpu.make_async_copy(dst, dst, sem).wait()

    def start1(d):
        for dd in (d, NZ - d) if d < NZ // 2 else (d,):
            p = lax.rem(z + dd, NZ)
            z_slot(p).start()
            z_down1(p).start()

    def ring_z(d):
        return [lax.rem(z + dd, NZ) for dd in ((d, NZ - d) if d < NZ // 2 else (d,))]

    def start1(d):
        for p in ring_z(d):
            z_slot(p).start()
            z_down1(p).start()

    def start_up(d):
        for p in ring_z(d):
            z_up1(p).start()

    for q in range(4):
        swap_h(q).start()
    swap_w(blk(2, 2)).start()
    start1(1)
    for ox, oy in BLOCK_ORDER[1:7]:
        swap_w(blk(ox, oy)).start()
    hear_z(0)
    tell(ready_z.at[1], near_z)
    start1(2)
    for ox, oy in BLOCK_ORDER[7:]:
        swap_w(blk(ox, oy)).start()

    def product(q, b):
        r = pl.ds(pl.multiple_of(q * 256, 256), 256)
        return jnp.dot(h_own[r, :], w_own[b], preferred_element_type=F32) + jnp.dot(
            h_sib[r, :], w_sib[b], preferred_element_type=F32
        )

    def order(j):
        return jnp.where(j == 0, 2, jnp.where(j == 1, 1, jnp.where(j == 2, 3, 0)))

    def block_of(f, along, across):
        first = f // 2 == 0
        return blk(jnp.where(first, along, across), jnp.where(first, across, along))

    def ahead(f):
        return jnp.where(lax.rem(f, 2) == 0, 1, 3)

    def other(f):
        return f + 1 - 2 * lax.rem(f, 2)

    def peer1(f):
        first = f // 2 == 0
        d = ahead(f)
        return at(x + jnp.where(first, d, 0), y + jnp.where(first, 0, d), core)

    def peer2(f):
        first = f // 2 == 0
        d = ahead(f)
        return at(x + jnp.where(first, 0, d), y + jnp.where(first, d, 0), core)

    def copy1(f, s, j):
        return remote(send1.at[f, s, j], recv1.at[f, s, j], s1_s.at[f, s, j], s1_r.at[f, s, j], peer1(f))

    def copy2(f, s):
        return remote(send2.at[f, s], recv2.at[f, s], s2_s.at[f, s], s2_r.at[f, s], peer2(f))

    for q in range(4):
        load_h(q).wait()
        swap_h(q).wait_recv()

    def need_w(b):
        load_w(b).wait()
        swap_w(b).wait_recv()

    def place(n):
        late = n - 4
        return (
            jnp.where(n < 4, 0, 1 + lax.rem(late, 2)),
            jnp.where(n < 4, n, late // 2),
        )

    def hold_back(f, n):
        @pl.when(n >= DEPTH)
        def _():
            s_, j_ = place(n - DEPTH)
            copy1(f, s_, j_).wait_send()

    def step0(i, _):
        j = i // 4
        f = lax.rem(i, 4)
        o = order(j)

        @pl.when(f == 0)
        def _():
            need_w(blk(2, o))

        @pl.when((f == 2) & (j > 0))
        def _():
            need_w(blk(o, 2))

        send1[f, 0, j] = product(f, block_of(f, 2, o)).astype(BF)
        hold_back(f, j)
        copy1(f, 0, j).start()
        return 0

    lax.fori_loop(0, 4, step0, 0)
    hear_z(1)
    tell(ready_z.at[2], near_z)
    start1(3)
    lax.fori_loop(4, 8, step0, 0)
    hear_z(2)
    start1(4)
    start_up(1)
    start_up(2)
    lax.fori_loop(8, 16, step0, 0)
    hear_plane(0)
    tell(ready_p.at[1], near_plane)
    for ox, oy in BLOCK_ORDER[7:]:
        need_w(blk(ox, oy))

    def both(j):
        def step1(f, _):
            send1[f, 1, j] = product(other(f), block_of(f, ahead(f), order(j))).astype(BF)
            hold_back(f, 4 + 2 * j)
            copy1(f, 1, j).start()
            return 0

        def step2(f, _):
            v = product(f, block_of(f, ahead(f), order(j)))
            copy1(f, 0, j).wait_recv()
            send1[f, 2, j] = (v + recv1[f, 0, j].astype(F32)).astype(BF)
            hold_back(f, 5 + 2 * j)
            copy1(f, 2, j).start()
            return 0

        lax.fori_loop(0, 4, step1, 0)
        lax.fori_loop(0, 4, step2, 0)

    def both_loop(j, _):
        both(j)
        return 0

    lax.fori_loop(0, 2, both_loop, 0)
    hear_plane(1)
    tell(ready_p.at[2], near_plane)

    def slot_copy(p):
        return pltpu.make_async_copy(slot_in.at[p], slot_s.at[p], slot_sem.at[p])

    own_slots = pltpu.make_async_copy(slot_out, slot_s.at[z], loc_sem.at[2])
    own_slots.start()

    def take_slots(p):
        got(slot_in.at[p], zs_r.at[p])
        slot_copy(p).start()

    each_z(take_slots)
    each_z(lambda p: slot_copy(p).wait())
    own_slots.wait()
    own_down.wait()
    each_z(lambda p: got(p_down.at[pl.ds(p * 8, 8)], zd1_r.at[p]))

    def choose(src, dst):
        def body_for(p):
            def body(i, _):
                dst[p, i] = src[slot_s[p, i, 0]]
                return 0
            lax.fori_loop(0, 8, body, 0)
        return body_for

    def send_down(p):
        choose(p_down, s_down)(p)
        z_down2(p).start()

    each_z(send_down)
    start_up(3)
    start_up(4)

    def keep_down(i, _):
        a_down[i, z] = p_down[slot_s[z, i, 0]]
        return 0

    def keep_up(i, _):
        a_up[i, z] = p_up[slot_s[z, i, 0]]
        return 0

    lax.fori_loop(0, 8, keep_down, 0)

    def step3(i, _):
        j = i // 4
        f = lax.rem(i, 4)
        part[f, j] = product(f, block_of(f, 0, order(j)))
        return 0

    lax.fori_loop(2, 3, both_loop, 0)
    hear_plane(2)
    tell(ready_p.at[3], near_plane)
    lax.fori_loop(0, 4, step3, 0)

    def total1(q, j):
        copy1(q, 2, j).wait_recv()
        copy1(other(q), 1, j).wait_recv()
        return part[q, j] + recv1[q, 2, j].astype(F32) + recv1[other(q), 1, j].astype(F32)

    def turn0(q, _):
        send2[q, 0] = total1(q, 0).astype(BF)
        copy2(q, 0).start()
        return 0

    lax.fori_loop(0, 4, turn0, 0)

    lax.fori_loop(3, 4, both_loop, 0)
    hear_plane(3)
    lax.fori_loop(4, 16, step3, 0)

    def turn1(i, _):
        j = 1 + i // 4
        q = lax.rem(i, 4)
        v = total1(q, j)
        keep = lax.rem(q, 2) == j - 1

        @pl.when(keep)
        def _():
            hold[q] = v

        @pl.when(jnp.logical_not(keep))
        def _():
            send2[other(q), 1] = v.astype(BF)
            copy2(other(q), 1).start()

        return 0

    lax.fori_loop(0, 8, turn1, 0)

    def turn2(q, _):
        v = hold[q]
        copy2(q, 0).wait_recv()
        send2[q, 2] = (v + recv2[q, 0].astype(F32)).astype(BF)
        copy2(q, 2).start()
        return 0

    lax.fori_loop(0, 4, turn2, 0)

    each_z(lambda p: got(a_down.at[:, p], zd2_r.at[p]))

    def rank(i, _):
        r = pl.ds(pl.multiple_of(i * 128, 128), 128)
        v = lax.dot_general(
            a_down[i].reshape(64, 640), h_own[r, :], (((1,), (1,)), ((), ())),
            preferred_element_type=F32,
        )
        rank_out[pl.ds(i * 4, 4)] = v.astype(BF).reshape(4, 16, 128)
        return 0

    lax.fori_loop(0, 8, rank, 0)

    def copy_a(p):
        return remote(rank_out.at[p], rank_in.at[t], ra_s.at[p], ra_r.at[t], at_t(p))

    def copy_b(p):
        return remote(rank_sum, rank_all.at[t], rb_s.at[p], rb_r.at[t], at_t(p))

    def each_t(make):
        def body(i, _):
            make(lax.rem(t + i, NTP))
            return 0
        lax.fori_loop(1, NTP, body, 0)

    each_t(lambda p: copy_a(p).start())

    def turn3(q, _):
        part[q, 3] = total1(q, 3)
        return 0

    for q in range(4):
        swap_h(q).wait_send()

    def sent_w(b, _):
        swap_w(b).wait_send()
        return 0

    lax.fori_loop(0, 16, sent_w, 0)

    def sent_z(p):
        z_slot(p).wait_send()
        z_down1(p).wait_send()
        z_up1(p).wait_send()
        z_down2(p).wait_send()

    each_z(sent_z)
    own_up.wait()
    each_z(lambda p: got(p_up.at[pl.ds(p * 8, 8)], zu1_r.at[p]))

    def send_up(p):
        choose(p_up, s_up)(p)
        z_up2(p).start()

    each_z(send_up)
    lax.fori_loop(0, 8, keep_up, 0)

    lax.fori_loop(0, 4, turn3, 0)
    each_t(lambda p: got(rank_in.at[p], ra_r.at[p]))

    def add_rank(i, acc):
        return acc + rank_in[lax.rem(t + i, NTP)].astype(F32)

    total = lax.fori_loop(1, NTP, add_rank, rank_out[t].astype(F32)).astype(BF)
    rank_sum[...] = total
    rank_all[t] = total
    each_t(lambda p: copy_b(p).start())
    each_z(lambda p: got(a_up.at[:, p], zu2_r.at[p]))
    each_t(lambda p: got(rank_all.at[p], rb_r.at[p]))

    def finish(q, _):
        copy2(q, 2).wait_recv()
        copy2(other(q), 1).wait_recv()
        base = part[q, 3] + recv2[q, 2].astype(F32) + recv2[other(q), 1].astype(F32)
        for k in range(2):
            i = q * 2 + k
            v = lax.dot_general(
                rank_all[pl.ds(i * 4, 4)].reshape(64, 128), a_up[i].reshape(64, 256),
                (((0,), (0,)), ((), ())), preferred_element_type=F32,
            )
            delta = (v * adapter_scale).astype(BF).astype(F32)
            r = pl.ds(pl.multiple_of(i * 128, 128), 128)
            out[r, :] = (base[k * 128:(k + 1) * 128] + delta).astype(BF)
        return 0

    lax.fori_loop(0, 4, finish, 0)

    def sent1(i, _):
        s_, j_ = place(12 - DEPTH + i // 4)
        copy1(lax.rem(i, 4), s_, j_).wait_send()
        return 0

    lax.fori_loop(0, 4 * DEPTH, sent1, 0)

    def sent2(i, _):
        copy2(i // 3, lax.rem(i, 3)).wait_send()
        return 0

    lax.fori_loop(0, 12, sent2, 0)

    each_z(lambda p: z_up2(p).wait_send())

    def sent_t(p):
        copy_a(p).wait_send()
        copy_b(p).wait_send()

    each_t(sent_t)


def local(hidden, down_weight, adapter_down_factor, adapter_up_factor, row_tile_adapter, adapter_pool_slot):
    any_ = pl.BlockSpec(memory_space=pl.ANY)
    smem = pl.BlockSpec(memory_space=pltpu.SMEM)
    V, D = pltpu.VMEM, pltpu.SemaphoreType.DMA
    down = adapter_down_factor.reshape(8, 8, 8, 640)
    up = adapter_up_factor.reshape(8, 8, 8, 256)
    return pl.pallas_call(
        kernel,
        out_shape=jax.ShapeDtypeStruct((1024, 256), BF),
        in_specs=[any_, any_, any_, any_, smem, smem],
        out_specs=pl.BlockSpec(memory_space=pltpu.VMEM),
        scratch_shapes=[
            V((1024, 640), BF), V((1024, 640), BF),
            V((16, 640, 256), BF), V((16, 640, 256), BF),
            V((4, 3, 4, 256, 256), BF), V((4, 3, 4, 256, 256), BF),
            V((4, 3, 256, 256), BF), V((4, 3, 256, 256), BF),
            V((4, 4, 256, 256), F32), V((4, 256, 256), F32),
            V((64, 8, 640), BF), V((8, 8, 8, 640), BF), V((8, 8, 8, 640), BF),
            V((64, 8, 256), BF), V((8, 8, 8, 256), BF), V((8, 8, 8, 256), BF),
            V((8, 128), jnp.int32), V((8, 8, 128), jnp.int32), pltpu.SMEM((8, 8, 128), jnp.int32),
            V((32, 16, 128), BF), V((32, 16, 128), BF), V((16, 128), BF), V((32, 16, 128), BF),
            D((20,)), D((4,)), D((4,)), D((16,)), D((16,)),
            D((4, 3, 4)), D((4, 3, 4)), D((4, 3)), D((4, 3)),
            D((8,)), D((8,)), D((8,)), D((8,)), D((8,)), D((8,)),
            D((8,)), D((8,)), D((8,)), D((8,)),
            D((32,)), D((32,)), D((32,)), D((32,)), D((3,)), D((8,)),
            pltpu.SemaphoreType.REGULAR((4,)), pltpu.SemaphoreType.REGULAR((3,)),
        ],
        compiler_params=pltpu.CompilerParams(
            collective_id=0, has_side_effects=True, vmem_limit_bytes=60 * 2**20
        ),
    )(hidden, down_weight, down, up, row_tile_adapter, adapter_pool_slot)


def solution(mesh):
    placed = (
        P("grp", "tp"), P("tp", None), P("grp", None, "tp"), P("grp", None, "tp"), P("grp"), P(),
    )
    return jax.shard_map(local, mesh=mesh, in_specs=placed, out_specs=P("grp", "tp"), check_vma=False)
```

```python
import jax
import jax.numpy as jnp
from jax import lax
from jax.experimental import pallas as pl
from jax.experimental.pallas import tpu as pltpu
from jax.sharding import PartitionSpec as P

adapter_scale = 2.0
MESH = pl.DeviceIdType.MESH
NX, NY, NZ, NTP = 4, 4, 8, 32
BF, F32 = jnp.bfloat16, jnp.float32
DEPTH = 4
CUT = 384
GROUPS = (
    ((2, 2),), ((2, 1), (1, 2)), ((2, 3), (3, 2)), ((2, 0), (0, 2)),
    ((1, 1), (1, 3), (3, 1), (3, 3), (1, 0), (3, 0), (0, 1), (0, 3), (0, 0)),
)


def kernel(
    hid, wgt, down, up, tiles, slots, out,
    h_own, h_sib, w_own, w_sib, send1, recv1, send2, recv2, part, hold,
    p_da, s_da, a_da, p_db, s_db, a_db, p_up, s_up, a_up, slot_out, slot_in, slot_s,
    rank_out, rank_in, rank_sum, rank_all,
    h_l, h_s, h_r, w_l, w_s, w_r, s1_s, s1_r, s2_s, s2_r, z_s, z_r, r_s, r_r, loc_sem,
    ready_p, ready_z,
):
    z = lax.axis_index("grp")
    t = lax.axis_index("tp")
    core = lax.rem(t, 2)
    y = lax.rem(t // 2, NY)
    x = t // (2 * NY)

    def at(xx, yy, cc):
        return {"grp": z, "tp": (lax.rem(xx, NX) * NY + lax.rem(yy, NY)) * 2 + cc}

    def at_z(zz):
        return {"grp": zz, "tp": t}

    def at_t(tt):
        return {"grp": z, "tp": tt}

    def remote(src, dst, ssem, rsem, dev):
        return pltpu.make_async_remote_copy(
            src_ref=src, dst_ref=dst, send_sem=ssem, recv_sem=rsem,
            device_id=dev, device_id_type=MESH,
        )

    def got(ref, sem):
        pltpu.make_async_copy(ref, ref, sem).wait()

    sib = at(x, y, 1 - core)

    def blk(ox, oy):
        return lax.rem(x + ox, NX) * NY + lax.rem(y + oy, NY)

    def load_h(q):
        r = pl.ds(q * 256, 256)
        return pltpu.make_async_copy(hid.at[r], h_own.at[r], h_l.at[q])

    def load_w(b, g):
        c = pl.multiple_of((2 * b + core) * 256, 256)
        return pltpu.make_async_copy(wgt.at[:, pl.ds(c, 256)], w_own.at[b], w_l.at[g])

    def swap_h(q):
        r = pl.ds(q * 256, 256)
        return remote(hid.at[r], h_sib.at[r], h_s, h_r.at[q], sib)

    def swap_w(b, g):
        c = pl.multiple_of((2 * b + 1 - core) * 256, 256)
        return remote(wgt.at[:, pl.ds(c, 256)], w_sib.at[b], w_s, w_r.at[g], sib)

    for q in range(4):
        load_h(q).start()
    for g, group in enumerate(GROUPS):
        for ox, oy in group:
            load_w(blk(ox, oy), g).start()

    row = lax.broadcasted_iota(jnp.int32, (8, 128), 0)
    mine = jnp.zeros((8, 128), jnp.int32)
    for i in range(8):
        mine = jnp.where(row == i, slots[tiles[i]], mine)
    slot_out[...] = mine

    barrier = pltpu.get_barrier_semaphore()
    near_plane = [sib] + [at(x + d, y, core) for d in (1, 3)] + [at(x, y + d, core) for d in (1, 3)]
    near_z = [at_z(lax.rem(z + d, NZ)) for d in (1, NZ - 1)]

    def tell(sem, devices):
        for dev in devices:
            pl.semaphore_signal(sem, inc=1, device_id=dev, device_id_type=MESH)

    tell(barrier, near_plane + near_z)
    pl.semaphore_wait(barrier, 7)

    def hear_plane(k):
        pl.semaphore_wait(ready_p.at[k], 5)

    def hear_z(k):
        pl.semaphore_wait(ready_z.at[k], 2)

    LA, LB = pl.ds(0, CUT), pl.ds(CUT, 640 - CUT)

    def ends(n, p):
        mine_at = pl.ds(z * 8, 8)
        return (
            (slot_out, slot_in.at[z]),
            (down.at[:, p, :, LA], p_da.at[mine_at]),
            (down.at[:, p, :, LB], p_db.at[mine_at]),
            (up.at[:, p], p_up.at[mine_at]),
            (s_da.at[p], a_da.at[:, z]),
            (s_db.at[p], a_db.at[:, z]),
            (s_up.at[p], a_up.at[:, z]),
        )[n]

    whole = (slot_in, p_da, p_db, p_up, a_da, a_db, a_up)
    others = (
        slot_in.at[pl.ds(0, 7)], p_da.at[pl.ds(0, 56)], p_db.at[pl.ds(0, 56)], p_up.at[pl.ds(0, 56)],
        s_da.at[pl.ds(0, 7)], s_db.at[pl.ds(0, 7)], s_up.at[pl.ds(0, 7)],
    )

    def z_send(n, p):
        src, dst = ends(n, p)
        remote(src, dst, z_s.at[n], z_r.at[n], at_z(p)).start()

    def z_keep(n):
        src, dst = ends(n, z)
        pltpu.make_async_copy(src, dst, z_r.at[n]).start()

    def z_got(n):
        got(whole[n], z_r.at[n])

    def z_sent(n):
        got(others[n], z_s.at[n])

    def ring_z(d):
        return [lax.rem(z + dd, NZ) for dd in ((d, NZ - d) if d < NZ // 2 else (d,))]

    def start1(d):
        for n in (0, 1, 2):
            for p in ring_z(d):
                z_send(n, p)

    tell(ready_z.at[0], near_z)
    swap_h(0).start()
    swap_w(blk(2, 2), 0).start()
    for q in range(1, 4):
        swap_h(q).start()
    start1(1)
    for g in (1, 2, 3):
        for ox, oy in GROUPS[g]:
            swap_w(blk(ox, oy), g).start()
    tell(ready_p.at[0], near_plane)
    for n in (0, 1, 2, 3):
        z_keep(n)
    hear_z(0)
    tell(ready_z.at[1], near_z)
    start1(2)
    for ox, oy in GROUPS[4]:
        swap_w(blk(ox, oy), 4).start()

    def product(q, b):
        r = pl.ds(pl.multiple_of(q * 256, 256), 256)
        return jnp.dot(h_own[r, :], w_own[b], preferred_element_type=F32) + jnp.dot(
            h_sib[r, :], w_sib[b], preferred_element_type=F32
        )

    def order(j):
        return jnp.where(j == 0, 2, jnp.where(j == 1, 1, jnp.where(j == 2, 3, 0)))

    def block_of(f, along, across):
        first = f // 2 == 0
        return blk(jnp.where(first, along, across), jnp.where(first, across, along))

    def ahead(f):
        return jnp.where(lax.rem(f, 2) == 0, 1, 3)

    def other(f):
        return f + 1 - 2 * lax.rem(f, 2)

    def peer1(f):
        first = f // 2 == 0
        d = ahead(f)
        return at(x + jnp.where(first, d, 0), y + jnp.where(first, 0, d), core)

    def peer2(f):
        first = f // 2 == 0
        d = ahead(f)
        return at(x + jnp.where(first, 0, d), y + jnp.where(first, d, 0), core)

    def send_1(f, s, j, n):
        @pl.when(n >= DEPTH)
        def _():
            got(send1.at[0, 0, 0], s1_s.at[f, lax.rem(n, DEPTH)])

        rsem = s1_r.at[0, f, j] if s == 0 else s1_r.at[1, other(f) if s == 1 else f, j]
        remote(
            send1.at[f, s, j], recv1.at[f, s, j], s1_s.at[f, lax.rem(n, DEPTH)], rsem, peer1(f)
        ).start()

    def send_2(f, s):
        rsem = s2_r.at[0, f] if s == 0 else s2_r.at[1, other(f) if s == 1 else f]
        remote(send2.at[f, s], recv2.at[f, s], s2_s, rsem, peer2(f)).start()

    def need_w(g, n):
        got(w_own.at[pl.ds(0, n)], w_l.at[g])
        got(w_sib.at[pl.ds(0, n)], w_r.at[g])

    def step0(i, _):
        j = i // 4
        f = lax.rem(i, 4)

        @pl.when(j == 0)
        def _():
            got(h_own.at[pl.ds(0, 256)], h_l.at[f])
            got(h_sib.at[pl.ds(0, 256)], h_r.at[f])

        @pl.when(i == 0)
        def _():
            need_w(0, 1)

        @pl.when((f == 0) & (j > 0))
        def _():
            need_w(j, 2)

        send1[f, 0, j] = product(f, block_of(f, 2, order(j))).astype(BF)
        send_1(f, 0, j, j)
        return 0

    lax.fori_loop(0, 4, step0, 0)
    hear_z(1)
    tell(ready_z.at[2], near_z)
    start1(3)
    lax.fori_loop(4, 8, step0, 0)
    hear_z(2)
    start1(4)
    lax.fori_loop(8, 16, step0, 0)
    hear_plane(0)
    tell(ready_p.at[1], near_plane)
    need_w(4, 9)

    def both(j, _):
        def step1(f, _):
            send1[f, 1, j] = product(other(f), block_of(f, ahead(f), order(j))).astype(BF)
            send_1(f, 1, j, 4 + 2 * j)
            return 0

        def step2(f, _):
            v = product(f, block_of(f, ahead(f), order(j)))
            got(recv1.at[f, 0, j], s1_r.at[0, f, j])
            send1[f, 2, j] = (v + recv1[f, 0, j].astype(F32)).astype(BF)
            send_1(f, 2, j, 5 + 2 * j)
            return 0

        lax.fori_loop(0, 4, step1, 0)
        lax.fori_loop(0, 4, step2, 0)
        return 0

    def step3(i, _):
        j = i // 4
        f = lax.rem(i, 4)
        part[f, j] = product(f, block_of(f, 0, order(j)))
        return 0

    def total1(q, j):
        got(recv1.at[q, pl.ds(1, 2), j], s1_r.at[1, q, j])
        return part[q, j] + recv1[q, 2, j].astype(F32) + recv1[other(q), 1, j].astype(F32)

    def turn0(q, _):
        send2[q, 0] = total1(q, 0).astype(BF)
        send_2(q, 0)
        return 0

    def turn1(i, _):
        j = 1 + i // 4
        q = lax.rem(i, 4)
        v = total1(q, j)
        keep = lax.rem(q, 2) == j - 1

        @pl.when(keep)
        def _():
            hold[q] = v

        @pl.when(jnp.logical_not(keep))
        def _():
            send2[other(q), 1] = v.astype(BF)
            send_2(other(q), 1)

        return 0

    def turn2(q, _):
        v = hold[q]
        got(recv2.at[q, 0], s2_r.at[0, q])
        send2[q, 2] = (v + recv2[q, 0].astype(F32)).astype(BF)
        send_2(q, 2)
        return 0

    def turn3(q, _):
        part[q, 3] = total1(q, 3)
        return 0

    def pick(n, src, dst):
        def one(p):
            def body(i, _):
                dst[p, i] = src[slot_s[p, i, 0]]
                return 0
            lax.fori_loop(0, 8, body, 0)

        def send(i, _):
            p = lax.rem(z + i, NZ)
            one(p)
            z_send(n, p)
            return 0

        lax.fori_loop(1, NZ, send, 0)
        one(z)
        z_keep(n)

    lax.fori_loop(0, 1, both, 0)
    z_got(0)
    cp = pltpu.make_async_copy(slot_in, slot_s, loc_sem)
    cp.start()
    hear_plane(1)
    tell(ready_p.at[2], near_plane)
    cp.wait()
    z_got(1)
    pick(4, p_da, s_da)
    lax.fori_loop(1, 2, both, 0)
    z_got(2)
    pick(5, p_db, s_db)

    def start_up(i, _):
        z_send(3, lax.rem(z + i, NZ))
        return 0

    lax.fori_loop(1, NZ, start_up, 0)
    lax.fori_loop(2, 3, both, 0)
    hear_plane(2)
    tell(ready_p.at[3], near_plane)
    lax.fori_loop(0, 4, step3, 0)
    lax.fori_loop(0, 4, turn0, 0)
    lax.fori_loop(3, 4, both, 0)
    hear_plane(3)
    lax.fori_loop(4, 8, step3, 0)
    lax.fori_loop(0, 4, turn1, 0)
    lax.fori_loop(8, 16, step3, 0)

    z_got(4)
    z_got(5)
    nt = (((1,), (1,)), ((), ()))
    for i in range(8):
        r = pl.ds(i * 128, 128)
        v = lax.dot_general(
            a_da[i].reshape(64, CUT), h_own[r, 0:CUT], nt, preferred_element_type=F32
        ) + lax.dot_general(
            a_db[i].reshape(64, 640 - CUT), h_own[r, CUT:640], nt, preferred_element_type=F32
        )
        rank_out[pl.ds(i * 4, 4)] = v.astype(BF).reshape(4, 16, 128)

    def send_a(i, _):
        p = lax.rem(t + i, NTP)
        remote(rank_out.at[p], rank_in.at[t], r_s.at[0], r_r.at[0], at_t(p)).start()
        return 0

    def send_b(i, _):
        p = lax.rem(t + i, NTP)
        remote(rank_sum, rank_all.at[t], r_s.at[1], r_r.at[1], at_t(p)).start()
        return 0

    lax.fori_loop(1, NTP, send_a, 0)
    pltpu.make_async_copy(rank_out.at[t], rank_in.at[t], r_r.at[0]).start()
    lax.fori_loop(4, 8, turn1, 0)
    lax.fori_loop(0, 4, turn2, 0)

    got(h_sib, h_s)
    got(w_sib, w_s)
    for n in range(6):
        z_sent(n)
    z_got(3)
    pick(6, p_up, s_up)
    lax.fori_loop(0, 4, turn3, 0)
    got(rank_in, r_r.at[0])

    def add_rank(i, acc):
        return acc + rank_in[i].astype(F32)

    rank_sum[...] = lax.fori_loop(0, NTP, add_rank, jnp.zeros((16, 128), F32)).astype(BF)
    lax.fori_loop(1, NTP, send_b, 0)
    pltpu.make_async_copy(rank_sum, rank_all.at[t], r_r.at[1]).start()

    def last_base(q, _):
        got(recv2.at[q, pl.ds(1, 2)], s2_r.at[1, q])
        part[q, 3] = part[q, 3] + recv2[q, 2].astype(F32) + recv2[other(q), 1].astype(F32)
        return 0

    lax.fori_loop(0, 4, last_base, 0)

    def sent1(i, _):
        got(send1.at[0, 0, 0], s1_s.at[lax.rem(i, 4), i // 4])
        return 0

    lax.fori_loop(0, 4 * DEPTH, sent1, 0)
    got(send2, s2_s)
    got(rank_in.at[pl.ds(0, NTP - 1)], r_s.at[0])
    z_sent(6)
    z_got(6)
    got(rank_all, r_r.at[1])

    def finish(q, _):
        for k in range(2):
            i = q * 2 + k
            v = lax.dot_general(
                rank_all[pl.ds(i * 4, 4)].reshape(64, 128), a_up[i].reshape(64, 256),
                (((0,), (0,)), ((), ())), preferred_element_type=F32,
            )
            delta = (v * adapter_scale).astype(BF).astype(F32)
            r = pl.ds(pl.multiple_of(i * 128, 128), 128)
            out[r, :] = (part[q, 3, k * 128:(k + 1) * 128] + delta).astype(BF)
        return 0

    lax.fori_loop(0, 4, finish, 0)
    got(rank_in.at[pl.ds(0, NTP - 1)], r_s.at[1])


def local(hidden, down_weight, adapter_down_factor, adapter_up_factor, row_tile_adapter, adapter_pool_slot):
    any_ = pl.BlockSpec(memory_space=pl.ANY)
    smem = pl.BlockSpec(memory_space=pltpu.SMEM)
    V, D = pltpu.VMEM, pltpu.SemaphoreType.DMA
    down = adapter_down_factor.reshape(8, 8, 8, 640)
    up = adapter_up_factor.reshape(8, 8, 8, 256)
    return pl.pallas_call(
        kernel,
        out_shape=jax.ShapeDtypeStruct((1024, 256), BF),
        in_specs=[any_, any_, any_, any_, smem, smem],
        out_specs=pl.BlockSpec(memory_space=pltpu.VMEM),
        scratch_shapes=[
            V((1024, 640), BF), V((1024, 640), BF),
            V((16, 640, 256), BF), V((16, 640, 256), BF),
            V((4, 3, 4, 256, 256), BF), V((4, 3, 4, 256, 256), BF),
            V((4, 3, 256, 256), BF), V((4, 3, 256, 256), BF),
            V((4, 4, 256, 256), F32), V((4, 256, 256), F32),
            V((64, 8, CUT), BF), V((8, 8, 8, CUT), BF), V((8, 8, 8, CUT), BF),
            V((64, 8, 640 - CUT), BF), V((8, 8, 8, 640 - CUT), BF), V((8, 8, 8, 640 - CUT), BF),
            V((64, 8, 256), BF), V((8, 8, 8, 256), BF), V((8, 8, 8, 256), BF),
            V((8, 128), jnp.int32), V((8, 8, 128), jnp.int32), pltpu.SMEM((8, 8, 128), jnp.int32),
            V((32, 16, 128), BF), V((32, 16, 128), BF), V((16, 128), BF), V((32, 16, 128), BF),
            D((4,)), D, D((4,)), D((5,)), D, D((5,)),
            D((4, DEPTH)), D((2, 4, 4)), D, D((2, 4)), D((7,)), D((7,)), D((2,)), D((2,)), D,
            pltpu.SemaphoreType.REGULAR((4,)), pltpu.SemaphoreType.REGULAR((3,)),
        ],
        compiler_params=pltpu.CompilerParams(
            collective_id=0, has_side_effects=True, vmem_limit_bytes=60 * 2**20
        ),
    )(hidden, down_weight, down, up, row_tile_adapter, adapter_pool_slot)


def solution(mesh):
    placed = (
        P("grp", "tp"), P("tp", None), P("grp", None, "tp"), P("grp", None, "tp"), P("grp"), P(),
    )
    return jax.shard_map(local, mesh=mesh, in_specs=placed, out_specs=P("grp", "tp"), check_vma=False)
```

```python
import jax
import jax.numpy as jnp
from jax import lax
from jax.experimental import pallas as pl
from jax.experimental.pallas import tpu as pltpu
from jax.sharding import PartitionSpec as P

adapter_scale = 2.0
MESH = pl.DeviceIdType.MESH
NX, NY, NZ, NTP = 4, 4, 8, 32
BF, F32 = jnp.bfloat16, jnp.float32
CUT = 384
GROUPS = (
    ((2, 2),), ((2, 1), (1, 2)), ((2, 3), (3, 2)), ((2, 0), (0, 2)),
    ((1, 1), (1, 3), (3, 1), (3, 3), (1, 0), (3, 0), (0, 1), (0, 3), (0, 0)),
)


def kernel(
    hid, wgt, down, up, tiles, slots, out,
    h_own, h_sib, w_own, w_sib, send1, recv1, send2, recv2, part, hold,
    p_da, s_da, a_da, p_db, s_db, a_db, p_up, s_up, a_up, slot_out, slot_in, slot_s,
    rank_out, rank_in, rank_sum, rank_all, delta,
    h_l, h_s, h_r, w_l, w_s, w_r, s1_s, s1_r, s2_s, s2_r, z_s, z_r, r_s, r_r, loc_sem,
    ready_p, ready_z,
):
    z = lax.axis_index("grp")
    t = lax.axis_index("tp")
    core = lax.rem(t, 2)
    y = lax.rem(t // 2, NY)
    x = t // (2 * NY)

    def at(xx, yy, cc):
        return {"grp": z, "tp": (lax.rem(xx, NX) * NY + lax.rem(yy, NY)) * 2 + cc}

    def at_z(zz):
        return {"grp": zz, "tp": t}

    def at_t(tt):
        return {"grp": z, "tp": tt}

    def remote(src, dst, ssem, rsem, dev):
        return pltpu.make_async_remote_copy(
            src_ref=src, dst_ref=dst, send_sem=ssem, recv_sem=rsem,
            device_id=dev, device_id_type=MESH,
        )

    def got(ref, sem):
        pltpu.make_async_copy(ref, ref, sem).wait()

    sib = at(x, y, 1 - core)

    def blk(ox, oy):
        return lax.rem(x + ox, NX) * NY + lax.rem(y + oy, NY)

    def load_h(q):
        r = pl.ds(q * 256, 256)
        return pltpu.make_async_copy(hid.at[r], h_own.at[r], h_l.at[q])

    def load_w(b, g):
        c = pl.multiple_of((2 * b + core) * 256, 256)
        return pltpu.make_async_copy(wgt.at[:, pl.ds(c, 256)], w_own.at[b], w_l.at[g])

    def swap_h(q):
        r = pl.ds(q * 256, 256)
        return remote(hid.at[r], h_sib.at[r], h_s, h_r.at[q], sib)

    def swap_w(b, g):
        c = pl.multiple_of((2 * b + 1 - core) * 256, 256)
        return remote(wgt.at[:, pl.ds(c, 256)], w_sib.at[b], w_s, w_r.at[g], sib)

    barrier = pltpu.get_barrier_semaphore()
    near_plane = [sib] + [at(x + d, y, core) for d in (1, 3)] + [at(x, y + d, core) for d in (1, 3)]
    near_z = [at_z(lax.rem(z + d, NZ)) for d in (1, NZ - 1)]

    def tell(sem, devices):
        for dev in devices:
            pl.semaphore_signal(sem, inc=1, device_id=dev, device_id_type=MESH)

    tell(barrier, near_plane + near_z)
    for q in range(4):
        load_h(q).start()
    for g, group in enumerate(GROUPS):
        for ox, oy in group:
            load_w(blk(ox, oy), g).start()

    row = lax.broadcasted_iota(jnp.int32, (8, 128), 0)
    mine = jnp.zeros((8, 128), jnp.int32)
    for i in range(8):
        mine = jnp.where(row == i, slots[tiles[i]], mine)
    slot_out[...] = mine

    pl.semaphore_wait(barrier, 7)

    def hear_plane(k):
        pl.semaphore_wait(ready_p.at[k], 5)

    def hear_z(k):
        pl.semaphore_wait(ready_z.at[k], 2)

    LA, LB = pl.ds(0, CUT), pl.ds(CUT, 640 - CUT)

    def ends(n, p):
        mine_at = pl.ds(z * 8, 8)
        return (
            (slot_out, slot_in.at[z]),
            (down.at[:, p, :, LA], p_da.at[mine_at]),
            (down.at[:, p, :, LB], p_db.at[mine_at]),
            (up.at[:, p], p_up.at[mine_at]),
            (s_da.at[2 * p + core], a_da.at[:, 0, z]),
            (s_db.at[2 * p + core], a_db.at[:, 0, z]),
            (s_up.at[p], a_up.at[:, z]),
        )[n]

    whole = (slot_in, p_da, p_db, p_up, a_da, a_db, a_up)
    others = (
        slot_in.at[pl.ds(0, 7)], p_da.at[pl.ds(0, 56)], p_db.at[pl.ds(0, 56)], p_up.at[pl.ds(0, 56)],
        s_da.at[pl.ds(0, 15)], s_db.at[pl.ds(0, 15)], s_up.at[pl.ds(0, 7)],
    )

    def z_send(n, p):
        src, dst = ends(n, p)
        remote(src, dst, z_s.at[n], z_r.at[n], at_z(p)).start()

    def z_keep(n):
        src, dst = ends(n, z)
        pltpu.make_async_copy(src, dst, z_r.at[n]).start()

    def z_cross(n, p):
        src = (s_da if n == 4 else s_db).at[2 * p + 1 - core]
        dst = (a_da if n == 4 else a_db).at[:, 1, z]
        dev = {"grp": p, "tp": t + 1 - 2 * core}
        remote(src, dst, z_s.at[n], z_r.at[n], dev).start()

    def z_got(n):
        got(whole[n], z_r.at[n])

    def z_sent(n):
        got(others[n], z_s.at[n])

    def ring_z(d):
        return [lax.rem(z + dd, NZ) for dd in ((d, NZ - d) if d < NZ // 2 else (d,))]

    def start1(d, which):
        for n in which:
            for p in ring_z(d):
                z_send(n, p)

    tell(ready_z.at[0], near_z)
    swap_h(0).start()
    swap_w(blk(2, 2), 0).start()
    for q in range(1, 4):
        swap_h(q).start()
    start1(1, (0, 1, 2))
    for g in (1, 2, 3):
        for ox, oy in GROUPS[g]:
            swap_w(blk(ox, oy), g).start()
    tell(ready_p.at[0], near_plane)
    for n in (0, 1, 2, 3):
        z_keep(n)
    hear_z(0)
    tell(ready_z.at[1], near_z)
    start1(2, (0, 1))
    for ox, oy in GROUPS[4]:
        swap_w(blk(ox, oy), 4).start()

    def product(q, b):
        r = pl.ds(pl.multiple_of(q * 256, 256), 256)
        return jnp.dot(h_own[r, :], w_own[b], preferred_element_type=F32) + jnp.dot(
            h_sib[r, :], w_sib[b], preferred_element_type=F32
        )

    def order(j):
        return jnp.where(j == 0, 2, jnp.where(j == 1, 1, jnp.where(j == 2, 3, 0)))

    def block_of(f, along, across):
        first = f // 2 == 0
        return blk(jnp.where(first, along, across), jnp.where(first, across, along))

    def ahead(f):
        return jnp.where(lax.rem(f, 2) == 0, 1, 3)

    def other(f):
        return f + 1 - 2 * lax.rem(f, 2)

    def peer1(f):
        first = f // 2 == 0
        d = ahead(f)
        return at(x + jnp.where(first, d, 0), y + jnp.where(first, 0, d), core)

    def peer2(f):
        first = f // 2 == 0
        d = ahead(f)
        return at(x + jnp.where(first, 0, d), y + jnp.where(first, d, 0), core)

    def send_1(f, s, j):
        rsem = s1_r.at[0 if s == 0 else 1, j]
        remote(send1.at[f, s, j], recv1.at[f, s, j], s1_s, rsem, peer1(f)).start()

    def send_2(f, s):
        rsem = s2_r.at[4] if s == 0 else s2_r.at[other(f) if s == 1 else f]
        remote(send2.at[f, s], recv2.at[f, s], s2_s, rsem, peer2(f)).start()

    def need_w(g, n):
        got(w_own.at[pl.ds(0, n)], w_l.at[g])
        got(w_sib.at[pl.ds(0, n)], w_r.at[g])

    def step0(i, _):
        j = i // 4
        f = lax.rem(i, 4)

        @pl.when(j == 0)
        def _():
            got(h_own.at[pl.ds(0, 256)], h_l.at[f])
            got(h_sib.at[pl.ds(0, 256)], h_r.at[f])

        @pl.when(i == 0)
        def _():
            need_w(0, 1)

        @pl.when((f == 0) & (j > 0))
        def _():
            need_w(j, 2)

        send1[f, 0, j] = product(f, block_of(f, 2, order(j))).astype(BF)
        send_1(f, 0, j)
        return 0

    lax.fori_loop(0, 3, step0, 0)
    hear_z(1)
    tell(ready_z.at[2], near_z)
    start1(3, (0, 1))
    lax.fori_loop(3, 6, step0, 0)
    hear_z(2)
    start1(4, (0, 1))
    start1(2, (2,))
    start1(3, (2,))
    start1(4, (2,))
    lax.fori_loop(6, 16, step0, 0)
    hear_plane(0)
    tell(ready_p.at[1], near_plane)
    need_w(4, 9)

    def near1(i, _):
        j = i // 4
        f = lax.rem(i, 4)
        send1[f, 1, j] = product(other(f), block_of(f, ahead(f), order(j))).astype(BF)
        send_1(f, 1, j)
        return 0

    def near2(i, _):
        j = i // 4
        f = lax.rem(i, 4)
        v = product(f, block_of(f, ahead(f), order(j)))
        @pl.when(f == 0)
        def _():
            got(recv1.at[:, 0, j], s1_r.at[0, j])

        send1[f, 2, j] = (v + recv1[f, 0, j].astype(F32)).astype(BF)
        send_1(f, 2, j)
        return 0

    def step3(i, _):
        j = i // 4
        f = lax.rem(i, 4)
        part[f, j] = product(f, block_of(f, 0, order(j)))
        return 0

    def total1(q, j):
        @pl.when(q == 0)
        def _():
            got(recv1.at[:, pl.ds(1, 2), j], s1_r.at[1, j])

        return part[q, j] + recv1[q, 2, j].astype(F32) + recv1[other(q), 1, j].astype(F32)

    def turn0(q, _):
        send2[q, 0] = total1(q, 0).astype(BF)
        send_2(q, 0)
        return 0

    def turn1(i, _):
        j = 1 + i // 4
        q = lax.rem(i, 4)
        v = total1(q, j)
        keep = lax.rem(q, 2) == j - 1

        @pl.when(keep)
        def _():
            hold[q] = v

        @pl.when(jnp.logical_not(keep))
        def _():
            send2[other(q), 1] = v.astype(BF)
            send_2(other(q), 1)

        return 0

    def turn2(q, _):
        v = hold[q]
        @pl.when(q == 0)
        def _():
            got(recv2.at[:, 0], s2_r.at[4])

        send2[q, 2] = (v + recv2[q, 0].astype(F32)).astype(BF)
        send_2(q, 2)
        return 0

    def turn3(q, _):
        part[q, 3] = total1(q, 3)
        return 0

    def pick(n, src, dst):
        def one(p):
            def body(i, _):
                v = src[slot_s[p, i, 0]]
                if n == 6:
                    dst[p, i] = v
                else:
                    dst[2 * p + lax.rem(i, 2), i // 2] = v
                return 0
            lax.fori_loop(0, 8, body, 0)

        def send(i, _):
            p = lax.rem(z + i, NZ)
            one(p)
            z_send(n, p)
            if n != 6:
                z_cross(n, p)
            return 0

        lax.fori_loop(1, NZ, send, 0)
        one(z)
        z_keep(n)
        if n != 6:
            z_cross(n, z)

    lax.fori_loop(0, 4, near1, 0)
    z_got(0)
    cp = pltpu.make_async_copy(slot_in, slot_s, loc_sem)
    cp.start()
    hear_plane(1)
    tell(ready_p.at[2], near_plane)
    lax.fori_loop(0, 4, near2, 0)
    cp.wait()
    z_got(1)
    pick(4, p_da, s_da)
    lax.fori_loop(4, 8, near1, 0)
    lax.fori_loop(4, 8, near2, 0)
    z_got(2)
    pick(5, p_db, s_db)

    def start_up(i, _):
        z_send(3, lax.rem(z + i, NZ))
        return 0

    lax.fori_loop(1, NZ, start_up, 0)
    lax.fori_loop(8, 12, near1, 0)
    lax.fori_loop(8, 12, near2, 0)
    hear_plane(2)
    tell(ready_p.at[3], near_plane)
    lax.fori_loop(0, 4, step3, 0)
    lax.fori_loop(0, 4, turn0, 0)
    lax.fori_loop(4, 8, step3, 0)
    lax.fori_loop(0, 4, turn1, 0)
    hear_plane(3)
    lax.fori_loop(8, 16, step3, 0)

    z_got(4)
    z_got(5)
    nt = (((1,), (1,)), ((), ()))
    for m in range(4):
        r = pl.ds(pl.multiple_of((2 * m + core) * 128, 128), 128)
        v = jnp.zeros((64, 128), F32)
        for k, h in ((0, h_own), (1, h_sib)):
            v += lax.dot_general(
                a_da[m, k].reshape(64, CUT), h[r, 0:CUT], nt, preferred_element_type=F32
            ) + lax.dot_general(
                a_db[m, k].reshape(64, 640 - CUT), h[r, CUT:640], nt, preferred_element_type=F32
            )
        rank_out[pl.ds(m * 4, 4)] = v.astype(BF).reshape(4, 16, 128)

    chip = t // 2

    def send_a(i, _):
        p = lax.rem(chip + i, 16)
        remote(rank_out.at[p], rank_in.at[chip], r_s.at[0], r_r.at[0], at_t(2 * p + core)).start()
        return 0

    def send_b(i, _):
        p = lax.rem(chip + i, 16)
        remote(rank_sum, rank_all.at[0, chip], r_s.at[1], r_r.at[1], at_t(2 * p + core)).start()
        return 0

    lax.fori_loop(1, 16, send_a, 0)
    pltpu.make_async_copy(rank_out.at[chip], rank_in.at[chip], r_r.at[0]).start()
    lax.fori_loop(12, 16, near1, 0)
    lax.fori_loop(12, 16, near2, 0)
    z_got(3)
    pick(6, p_up, s_up)
    lax.fori_loop(4, 8, turn1, 0)
    got(rank_in, r_r.at[0])

    def add_rank(i, acc):
        return acc + rank_in[i].astype(F32)

    rank_sum[...] = lax.fori_loop(0, 16, add_rank, jnp.zeros((16, 128), F32)).astype(BF)
    lax.fori_loop(1, 16, send_b, 0)
    pltpu.make_async_copy(rank_sum, rank_all.at[0, chip], r_r.at[1]).start()
    lax.fori_loop(0, 4, turn2, 0)

    got(h_sib, h_s)
    got(w_sib, w_s)
    for n in range(6):
        z_sent(n)
    lax.fori_loop(0, 4, turn3, 0)

    got(rank_all.at[0], r_r.at[1])
    remote(rank_all.at[0], rank_all.at[1], r_s.at[2], r_r.at[2], sib).start()
    z_got(6)

    def adapt(half):
        for m in range(4):
            i = 2 * m + (core if half == 0 else 1 - core)
            v = lax.dot_general(
                rank_all[half, m * 4:m * 4 + 4].reshape(64, 128), a_up[i].reshape(64, 256),
                (((0,), (0,)), ((), ())), preferred_element_type=F32,
            )
            r = pl.ds(pl.multiple_of(lax.rem(i, 2) * 128, 128), 128)
            delta[m, r, :] = (v * adapter_scale).astype(BF).astype(F32)

    adapt(0)
    got(rank_all.at[1], r_r.at[2])
    adapt(1)
    got(send1, s1_s)
    got(rank_in.at[pl.ds(0, 15)], r_s.at[0])
    got(rank_in.at[pl.ds(0, 15)], r_s.at[1])
    got(rank_all.at[0], r_s.at[2])
    z_sent(6)

    def last(q, _):
        got(recv2.at[q, pl.ds(1, 2)], s2_r.at[q])
        v = part[q, 3] + recv2[q, 2].astype(F32) + recv2[other(q), 1].astype(F32) + delta[q]
        out[pl.ds(pl.multiple_of(q * 256, 256), 256), :] = v.astype(BF)
        return 0

    lax.fori_loop(0, 4, last, 0)
    got(send2, s2_s)


def local(hidden, down_weight, adapter_down_factor, adapter_up_factor, row_tile_adapter, adapter_pool_slot):
    any_ = pl.BlockSpec(memory_space=pl.ANY)
    smem = pl.BlockSpec(memory_space=pltpu.SMEM)
    V, D = pltpu.VMEM, pltpu.SemaphoreType.DMA
    down = adapter_down_factor.reshape(8, 8, 8, 640)
    up = adapter_up_factor.reshape(8, 8, 8, 256)
    return pl.pallas_call(
        kernel,
        out_shape=pltpu.VMEM((1024, 256), BF),
        in_specs=[any_, any_, any_, any_, smem, smem],
        out_specs=pl.BlockSpec(memory_space=pltpu.VMEM),
        scratch_shapes=[
            V((1024, 640), BF), V((1024, 640), BF),
            V((16, 640, 256), BF), V((16, 640, 256), BF),
            V((4, 3, 4, 256, 256), BF), V((4, 3, 4, 256, 256), BF),
            V((4, 3, 256, 256), BF), V((4, 3, 256, 256), BF),
            V((4, 4, 256, 256), F32), V((4, 256, 256), F32),
            V((64, 8, CUT), BF), V((16, 4, 8, CUT), BF), V((4, 2, 8, 8, CUT), BF),
            V((64, 8, 640 - CUT), BF), V((16, 4, 8, 640 - CUT), BF), V((4, 2, 8, 8, 640 - CUT), BF),
            V((64, 8, 256), BF), V((8, 8, 8, 256), BF), V((8, 8, 8, 256), BF),
            V((8, 128), jnp.int32), V((8, 8, 128), jnp.int32), pltpu.SMEM((8, 8, 128), jnp.int32),
            V((16, 16, 128), BF), V((16, 16, 128), BF), V((16, 128), BF), V((2, 16, 16, 128), BF), V((4, 256, 256), F32),
            D((4,)), D, D((4,)), D((5,)), D, D((5,)),
            D, D((2, 4)), D, D((5,)), D((7,)), D((7,)), D((3,)), D((3,)), D,
            pltpu.SemaphoreType.REGULAR((4,)), pltpu.SemaphoreType.REGULAR((3,)),
        ],
        compiler_params=pltpu.CompilerParams(
            collective_id=0, has_side_effects=True, vmem_limit_bytes=60 * 2**20
        ),
    )(hidden, down_weight, down, up, row_tile_adapter, adapter_pool_slot)


def solution(mesh):
    placed = (
        P("grp", "tp"), P("tp", None), P("grp", None, "tp"), P("grp", None, "tp"), P("grp"), P(),
    )
    return jax.shard_map(local, mesh=mesh, in_specs=placed, out_specs=P("grp", "tp"), check_vma=False)
```

```python
import jax
import jax.numpy as jnp
from jax import lax
from jax.experimental import pallas as pl
from jax.experimental.pallas import tpu as pltpu
from jax.sharding import PartitionSpec as P

adapter_scale = 2.0
MESH = pl.DeviceIdType.MESH
NX, NY, NZ, NTP = 4, 4, 8, 32
BF, F32 = jnp.bfloat16, jnp.float32
CUT = 384
GROUPS = (
    ((2, 2),), ((2, 1), (1, 2)), ((2, 3), (3, 2)), ((2, 0), (0, 2)),
    ((1, 1), (1, 3), (3, 1), (3, 3), (1, 0), (3, 0), (0, 1), (0, 3), (0, 0)),
)


def kernel(
    hid, wgt, down, up, tiles_any, slots_any, out, tiles, slots,
    h_own, h_sib, w_own, w_sib, send1, recv1, send2, recv2, part, hold,
    p_da, s_da, a_da, p_db, s_db, a_db, p_up, s_up, a_up, slot_out, slot_in, slot_s,
    rank_out, rank_in, rank_sum, rank_all, delta,
    h_l, h_s, h_r, w_l, w_s, w_r, s1_s, s1_r, s2_s, s2_r, z_s, z_r, r_s, r_r, loc_sem, t_sem,
    ready_p, ready_z,
):
    z = lax.axis_index("grp")
    t = lax.axis_index("tp")
    core = lax.rem(t, 2)
    y = lax.rem(t // 2, NY)
    x = t // (2 * NY)

    def at(xx, yy, cc):
        return {"grp": z, "tp": (lax.rem(xx, NX) * NY + lax.rem(yy, NY)) * 2 + cc}

    def at_z(zz):
        return {"grp": zz, "tp": t}

    def at_t(tt):
        return {"grp": z, "tp": tt}

    def remote(src, dst, ssem, rsem, dev):
        return pltpu.make_async_remote_copy(
            src_ref=src, dst_ref=dst, send_sem=ssem, recv_sem=rsem,
            device_id=dev, device_id_type=MESH,
        )

    def got(ref, sem):
        pltpu.make_async_copy(ref, ref, sem).wait()

    sib = at(x, y, 1 - core)

    def blk(ox, oy):
        return lax.rem(x + ox, NX) * NY + lax.rem(y + oy, NY)

    def load_h(q):
        r = pl.ds(q * 256, 256)
        return pltpu.make_async_copy(hid.at[r], h_own.at[r], h_l.at[q])

    def load_w(b, g):
        c = pl.multiple_of((2 * b + core) * 256, 256)
        return pltpu.make_async_copy(wgt.at[:, pl.ds(c, 256)], w_own.at[b], w_l.at[g])

    def swap_h(q):
        r = pl.ds(q * 256, 256)
        return remote(hid.at[r], h_sib.at[r], h_s, h_r.at[q], sib)

    def swap_w(b, g):
        c = pl.multiple_of((2 * b + 1 - core) * 256, 256)
        return remote(wgt.at[:, pl.ds(c, 256)], w_sib.at[b], w_s, w_r.at[g], sib)

    barrier = pltpu.get_barrier_semaphore()
    near_plane = [sib] + [at(x + d, y, core) for d in (1, 3)] + [at(x, y + d, core) for d in (1, 3)]
    near_z = [at_z(lax.rem(z + d, NZ)) for d in (1, NZ - 1)]

    def tell(sem, devices):
        for dev in devices:
            pl.semaphore_signal(sem, inc=1, device_id=dev, device_id_type=MESH)

    tell(barrier, near_plane + near_z)
    tables = [
        pltpu.make_async_copy(tiles_any, tiles, t_sem.at[0]),
        pltpu.make_async_copy(slots_any, slots, t_sem.at[1]),
    ]
    for cp in tables:
        cp.start()
    for q in range(4):
        load_h(q).start()
    for g, group in enumerate(GROUPS):
        for ox, oy in group:
            load_w(blk(ox, oy), g).start()

    pl.semaphore_wait(barrier, 7)

    def hear_plane(k):
        pl.semaphore_wait(ready_p.at[k], 5)

    def hear_z(k):
        pl.semaphore_wait(ready_z.at[k], 2)

    LA, LB = pl.ds(0, CUT), pl.ds(CUT, 640 - CUT)

    def ends(n, p):
        mine_at = pl.ds(z * 8, 8)
        return (
            (slot_out, slot_in.at[z]),
            (down.at[:, p, :, LA], p_da.at[mine_at]),
            (down.at[:, p, :, LB], p_db.at[mine_at]),
            (up.at[:, p], p_up.at[mine_at]),
            (s_da.at[2 * p + core], a_da.at[:, 0, z]),
            (s_db.at[2 * p + core], a_db.at[:, 0, z]),
            (s_up.at[p], a_up.at[:, z]),
        )[n]

    whole = (slot_in, p_da, p_db, p_up, a_da, a_db, a_up)
    others = (
        slot_in.at[pl.ds(0, 7)], p_da.at[pl.ds(0, 56)], p_db.at[pl.ds(0, 56)], p_up.at[pl.ds(0, 56)],
        s_da.at[pl.ds(0, 15)], s_db.at[pl.ds(0, 15)], s_up.at[pl.ds(0, 7)],
    )

    def z_send(n, p):
        src, dst = ends(n, p)
        remote(src, dst, z_s.at[n], z_r.at[n], at_z(p)).start()

    def z_keep(n):
        src, dst = ends(n, z)
        pltpu.make_async_copy(src, dst, z_r.at[n]).start()

    def z_cross(n, p):
        src = (s_da if n == 4 else s_db).at[2 * p + 1 - core]
        dst = (a_da if n == 4 else a_db).at[:, 1, z]
        dev = {"grp": p, "tp": t + 1 - 2 * core}
        remote(src, dst, z_s.at[n], z_r.at[n], dev).start()

    def z_got(n):
        got(whole[n], z_r.at[n])

    def z_sent(n):
        got(others[n], z_s.at[n])

    def ring_z(d):
        return [lax.rem(z + dd, NZ) for dd in ((d, NZ - d) if d < NZ // 2 else (d,))]

    def start1(d, which):
        for n in which:
            for p in ring_z(d):
                z_send(n, p)

    tell(ready_z.at[0], near_z)
    swap_h(0).start()
    swap_w(blk(2, 2), 0).start()
    for q in range(1, 4):
        swap_h(q).start()
    start1(1, (1, 2))
    for g in (1, 2, 3):
        for ox, oy in GROUPS[g]:
            swap_w(blk(ox, oy), g).start()
    tell(ready_p.at[0], near_plane)
    for n in (1, 2, 3):
        z_keep(n)
    for ox, oy in GROUPS[4]:
        swap_w(blk(ox, oy), 4).start()

    far = blk(2, 2)
    got(w_own.at[0], w_l.at[0])
    for f in range(4):
        got(h_own.at[pl.ds(0, 256)], h_l.at[f])
        part[f, 0] = jnp.dot(
            h_own[f * 256:(f + 1) * 256, :], w_own[far], preferred_element_type=F32
        )
    hear_z(0)
    tell(ready_z.at[1], near_z)
    start1(2, (1,))

    def product(q, b):
        r = pl.ds(pl.multiple_of(q * 256, 256), 256)
        return jnp.dot(h_own[r, :], w_own[b], preferred_element_type=F32) + jnp.dot(
            h_sib[r, :], w_sib[b], preferred_element_type=F32
        )

    def order(j):
        return jnp.where(j == 0, 2, jnp.where(j == 1, 1, jnp.where(j == 2, 3, 0)))

    def block_of(f, along, across):
        first = f // 2 == 0
        return blk(jnp.where(first, along, across), jnp.where(first, across, along))

    def ahead(f):
        return jnp.where(lax.rem(f, 2) == 0, 1, 3)

    def other(f):
        return f + 1 - 2 * lax.rem(f, 2)

    def peer1(f):
        first = f // 2 == 0
        d = ahead(f)
        return at(x + jnp.where(first, d, 0), y + jnp.where(first, 0, d), core)

    def peer2(f):
        first = f // 2 == 0
        d = ahead(f)
        return at(x + jnp.where(first, 0, d), y + jnp.where(first, d, 0), core)

    def send_1(f, s, j):
        rsem = s1_r.at[0 if s == 0 else 1, j]
        remote(send1.at[f, s, j], recv1.at[f, s, j], s1_s, rsem, peer1(f)).start()

    def send_2(f, s):
        rsem = s2_r.at[4] if s == 0 else s2_r.at[other(f) if s == 1 else f]
        remote(send2.at[f, s], recv2.at[f, s], s2_s, rsem, peer2(f)).start()

    def need_w(g, n):
        got(w_own.at[pl.ds(0, n)], w_l.at[g])
        got(w_sib.at[pl.ds(0, n)], w_r.at[g])

    got(w_sib.at[0], w_r.at[0])
    for f in range(4):
        got(h_sib.at[pl.ds(0, 256)], h_r.at[f])
        send1[f, 0, 0] = (
            part[f, 0]
            + jnp.dot(h_sib[f * 256:(f + 1) * 256, :], w_sib[far], preferred_element_type=F32)
        ).astype(BF)
        send_1(f, 0, 0)

    def step0(i, _):
        j = i // 4
        f = lax.rem(i, 4)

        @pl.when(f == 0)
        def _():
            need_w(j, 2)

        send1[f, 0, j] = product(f, block_of(f, 2, order(j))).astype(BF)
        send_1(f, 0, j)
        return 0

    hear_z(1)
    tell(ready_z.at[2], near_z)
    for cp in tables:
        cp.wait()
    row = lax.broadcasted_iota(jnp.int32, (8, 128), 0)
    mine = jnp.zeros((8, 128), jnp.int32)
    for i in range(8):
        mine = jnp.where(row == i, slots[tiles[i]], mine)
    slot_out[...] = mine

    z_keep(0)
    start1(3, (1,))
    lax.fori_loop(4, 7, step0, 0)
    hear_z(2)
    for d in (4, 3, 2, 1):
        start1(d, (0,))
    start1(4, (1,))
    start1(2, (2,))
    start1(3, (2,))
    start1(4, (2,))
    lax.fori_loop(7, 16, step0, 0)
    hear_plane(0)
    tell(ready_p.at[1], near_plane)
    need_w(4, 9)

    def near1(i, _):
        j = i // 4
        f = lax.rem(i, 4)
        send1[f, 1, j] = product(other(f), block_of(f, ahead(f), order(j))).astype(BF)
        send_1(f, 1, j)
        return 0

    def near2(i, _):
        j = i // 4
        f = lax.rem(i, 4)
        v = product(f, block_of(f, ahead(f), order(j)))
        @pl.when(f == 0)
        def _():
            got(recv1.at[:, 0, j], s1_r.at[0, j])

        send1[f, 2, j] = (v + recv1[f, 0, j].astype(F32)).astype(BF)
        send_1(f, 2, j)
        return 0

    def step3(i, _):
        j = i // 4
        f = lax.rem(i, 4)
        part[f, j] = product(f, block_of(f, 0, order(j)))
        return 0

    def total1(q, j):
        @pl.when(q == 0)
        def _():
            got(recv1.at[:, pl.ds(1, 2), j], s1_r.at[1, j])

        return part[q, j] + recv1[q, 2, j].astype(F32) + recv1[other(q), 1, j].astype(F32)

    def turn0(q, _):
        send2[q, 0] = total1(q, 0).astype(BF)
        send_2(q, 0)
        return 0

    def turn1(i, _):
        j = 1 + i // 4
        q = lax.rem(i, 4)
        v = total1(q, j)
        keep = lax.rem(q, 2) == j - 1

        @pl.when(keep)
        def _():
            hold[q] = v

        @pl.when(jnp.logical_not(keep))
        def _():
            send2[other(q), 1] = v.astype(BF)
            send_2(other(q), 1)

        return 0

    def turn2(q, _):
        v = hold[q]
        @pl.when(q == 0)
        def _():
            got(recv2.at[:, 0], s2_r.at[4])

        send2[q, 2] = (v + recv2[q, 0].astype(F32)).astype(BF)
        send_2(q, 2)
        return 0

    def turn3(q, _):
        part[q, 3] = total1(q, 3)
        return 0

    def pick(n, src, dst):
        def one(p):
            def body(i, _):
                v = src[slot_s[p, i, 0]]
                if n == 6:
                    dst[p, i] = v
                else:
                    dst[2 * p + lax.rem(i, 2), i // 2] = v
                return 0
            lax.fori_loop(0, 8, body, 0)

        def send(i, _):
            p = lax.rem(z + i, NZ)
            one(p)
            z_send(n, p)
            if n != 6:
                z_cross(n, p)
            return 0

        lax.fori_loop(1, NZ, send, 0)
        one(z)
        z_keep(n)
        if n != 6:
            z_cross(n, z)

    lax.fori_loop(0, 4, near1, 0)
    z_got(0)
    cp = pltpu.make_async_copy(slot_in, slot_s, loc_sem)
    cp.start()
    hear_plane(1)
    tell(ready_p.at[2], near_plane)
    lax.fori_loop(0, 4, near2, 0)
    cp.wait()
    z_got(1)
    pick(4, p_da, s_da)
    lax.fori_loop(4, 8, near1, 0)
    lax.fori_loop(4, 8, near2, 0)
    z_got(2)
    pick(5, p_db, s_db)

    def start_up(i, _):
        z_send(3, lax.rem(z + i, NZ))
        return 0

    lax.fori_loop(1, NZ, start_up, 0)
    lax.fori_loop(8, 12, near1, 0)
    lax.fori_loop(8, 12, near2, 0)
    hear_plane(2)
    tell(ready_p.at[3], near_plane)
    lax.fori_loop(0, 4, step3, 0)
    lax.fori_loop(0, 4, turn0, 0)
    lax.fori_loop(4, 8, step3, 0)
    lax.fori_loop(0, 4, turn1, 0)
    hear_plane(3)
    lax.fori_loop(8, 16, step3, 0)

    def near1_odd(i, _):
        return near1(13 + 2 * i, 0)

    def near1_even(i, _):
        return near1(12 + 2 * i, 0)

    lax.fori_loop(0, 2, near1_odd, 0)

    z_got(4)
    z_got(5)
    nt = (((1,), (1,)), ((), ()))
    for m in range(4):
        r = pl.ds(pl.multiple_of((2 * m + core) * 128, 128), 128)
        v = jnp.zeros((64, 128), F32)
        for k, h in ((0, h_own), (1, h_sib)):
            v += lax.dot_general(
                a_da[m, k].reshape(64, CUT), h[r, 0:CUT], nt, preferred_element_type=F32
            ) + lax.dot_general(
                a_db[m, k].reshape(64, 640 - CUT), h[r, CUT:640], nt, preferred_element_type=F32
            )
        rank_out[pl.ds(m * 4, 4)] = v.astype(BF).reshape(4, 16, 128)

    chip = t // 2

    def send_a(i, _):
        p = lax.rem(chip + i, 16)
        remote(rank_out.at[p], rank_in.at[chip], r_s.at[0], r_r.at[0], at_t(2 * p + core)).start()
        return 0

    def send_b(i, _):
        p = lax.rem(chip + i, 16)
        remote(rank_sum, rank_all.at[0, chip], r_s.at[1], r_r.at[1], at_t(2 * p + core)).start()
        return 0

    lax.fori_loop(1, 16, send_a, 0)
    pltpu.make_async_copy(rank_out.at[chip], rank_in.at[chip], r_r.at[0]).start()
    lax.fori_loop(0, 2, near1_even, 0)
    lax.fori_loop(12, 16, near2, 0)
    z_got(3)
    pick(6, p_up, s_up)
    lax.fori_loop(4, 8, turn1, 0)
    got(rank_in, r_r.at[0])

    def add_rank(i, acc):
        return acc + rank_in[i].astype(F32)

    rank_sum[...] = lax.fori_loop(0, 16, add_rank, jnp.zeros((16, 128), F32)).astype(BF)
    lax.fori_loop(1, 16, send_b, 0)
    pltpu.make_async_copy(rank_sum, rank_all.at[0, chip], r_r.at[1]).start()
    lax.fori_loop(0, 4, turn2, 0)

    got(h_sib, h_s)
    got(w_sib, w_s)
    for n in range(6):
        z_sent(n)
    lax.fori_loop(0, 4, turn3, 0)

    got(rank_all.at[0], r_r.at[1])
    remote(rank_all.at[0], rank_all.at[1], r_s.at[2], r_r.at[2], sib).start()
    z_got(6)

    def adapt(half):
        for m in range(4):
            i = 2 * m + (core if half == 0 else 1 - core)
            v = lax.dot_general(
                rank_all[half, m * 4:m * 4 + 4].reshape(64, 128), a_up[i].reshape(64, 256),
                (((0,), (0,)), ((), ())), preferred_element_type=F32,
            )
            r = pl.ds(pl.multiple_of(lax.rem(i, 2) * 128, 128), 128)
            delta[m, r, :] = (v * adapter_scale).astype(BF).astype(F32)

    adapt(0)
    got(rank_all.at[1], r_r.at[2])
    adapt(1)

    def last(q, _):
        got(recv2.at[q, pl.ds(1, 2)], s2_r.at[q])
        v = part[q, 3] + recv2[q, 2].astype(F32) + recv2[other(q), 1].astype(F32) + delta[q]
        out[pl.ds(pl.multiple_of(q * 256, 256), 256), :] = v.astype(BF)
        return 0

    lax.fori_loop(0, 4, last, 0)
    got(send1, s1_s)
    got(rank_in.at[pl.ds(0, 15)], r_s.at[0])
    got(rank_in.at[pl.ds(0, 15)], r_s.at[1])
    got(rank_all.at[0], r_s.at[2])
    z_sent(6)
    got(send2, s2_s)


def local(hidden, down_weight, adapter_down_factor, adapter_up_factor, row_tile_adapter, adapter_pool_slot):
    any_ = pl.BlockSpec(memory_space=pl.ANY)
    V, D = pltpu.VMEM, pltpu.SemaphoreType.DMA
    down = adapter_down_factor.reshape(8, 8, 8, 640)
    up = adapter_up_factor.reshape(8, 8, 8, 256)
    return pl.pallas_call(
        kernel,
        out_shape=pltpu.VMEM((1024, 256), BF),
        in_specs=[any_] * 6,
        out_specs=pl.BlockSpec(memory_space=pltpu.VMEM),
        scratch_shapes=[
            pltpu.SMEM((8,), jnp.int32), pltpu.SMEM((64,), jnp.int32),
            V((1024, 640), BF), V((1024, 640), BF),
            V((16, 640, 256), BF), V((16, 640, 256), BF),
            V((4, 3, 4, 256, 256), BF), V((4, 3, 4, 256, 256), BF),
            V((4, 3, 256, 256), BF), V((4, 3, 256, 256), BF),
            V((4, 4, 256, 256), F32), V((4, 256, 256), F32),
            V((64, 8, CUT), BF), V((16, 4, 8, CUT), BF), V((4, 2, 8, 8, CUT), BF),
            V((64, 8, 640 - CUT), BF), V((16, 4, 8, 640 - CUT), BF), V((4, 2, 8, 8, 640 - CUT), BF),
            V((64, 8, 256), BF), V((8, 8, 8, 256), BF), V((8, 8, 8, 256), BF),
            V((8, 128), jnp.int32), V((8, 8, 128), jnp.int32), pltpu.SMEM((8, 8, 128), jnp.int32),
            V((16, 16, 128), BF), V((16, 16, 128), BF), V((16, 128), BF), V((2, 16, 16, 128), BF), V((4, 256, 256), F32),
            D((4,)), D, D((4,)), D((5,)), D, D((5,)),
            D, D((2, 4)), D, D((5,)), D((7,)), D((7,)), D((3,)), D((3,)), D, D((2,)),
            pltpu.SemaphoreType.REGULAR((4,)), pltpu.SemaphoreType.REGULAR((3,)),
        ],
        compiler_params=pltpu.CompilerParams(
            collective_id=0, has_side_effects=True, vmem_limit_bytes=60 * 2**20
        ),
    )(hidden, down_weight, down, up, row_tile_adapter, adapter_pool_slot)


def solution(mesh):
    placed = (
        P("grp", "tp"), P("tp", None), P("grp", None, "tp"), P("grp", None, "tp"), P("grp"), P(),
    )
    return jax.shard_map(local, mesh=mesh, in_specs=placed, out_specs=P("grp", "tp"), check_vma=False)
```

```python
import jax
import jax.numpy as jnp
from jax import lax
from jax.experimental import pallas as pl
from jax.experimental.pallas import tpu as pltpu
from jax.sharding import PartitionSpec as P

adapter_scale = 2.0
MESH = pl.DeviceIdType.MESH
NX, NY, NZ, NTP = 4, 4, 8, 32
BF, F32 = jnp.bfloat16, jnp.float32
CUT = 384
GROUPS = (
    ((2, 2),), ((2, 1), (1, 2)), ((2, 3), (3, 2)), ((2, 0), (0, 2)),
    ((1, 1), (1, 3), (3, 1), (3, 3), (1, 0), (3, 0), (0, 1), (0, 3), (0, 0)),
)


def kernel(
    hid, wgt, down, up, tiles_any, slots_any, out, tiles, slots,
    h_own, h_sib, w_own, w_sib, send1, recv1, send2, recv2, part, hold,
    p_da, s_da, a_da, p_db, s_db, a_db, p_up, s_up, a_up, slot_out, slot_in, slot_s,
    rank_out, rank_in, rank_sum, rank_all, delta,
    h_l, h_s, h_r, w_l, w_s, w_r, s1_s, s1_r, s2_s, s2_r, z_s, z_r, r_s, r_r, loc_sem, t_sem,
    ready_p, ready_z,
):
    z = lax.axis_index("grp")
    t = lax.axis_index("tp")
    core = lax.rem(t, 2)
    y = lax.rem(t // 2, NY)
    x = t // (2 * NY)

    def at(xx, yy, cc):
        return {"grp": z, "tp": (lax.rem(xx, NX) * NY + lax.rem(yy, NY)) * 2 + cc}

    def at_z(zz):
        return {"grp": zz, "tp": t}

    def at_t(tt):
        return {"grp": z, "tp": tt}

    def remote(src, dst, ssem, rsem, dev):
        return pltpu.make_async_remote_copy(
            src_ref=src, dst_ref=dst, send_sem=ssem, recv_sem=rsem,
            device_id=dev, device_id_type=MESH,
        )

    def got(ref, sem):
        pltpu.make_async_copy(ref, ref, sem).wait()

    sib = at(x, y, 1 - core)

    def blk(ox, oy):
        return lax.rem(x + ox, NX) * NY + lax.rem(y + oy, NY)

    def load_h(q):
        r = pl.ds(q * 256, 256)
        return pltpu.make_async_copy(hid.at[r], h_own.at[r], h_l.at[q])

    def load_w(b, g):
        c = pl.multiple_of((2 * b + core) * 256, 256)
        return pltpu.make_async_copy(wgt.at[:, pl.ds(c, 256)], w_own.at[b], w_l.at[g])

    def swap_h(q):
        r = pl.ds(q * 256, 256)
        return remote(hid.at[r], h_sib.at[r], h_s, h_r.at[q], sib)

    def swap_w(b, g):
        c = pl.multiple_of((2 * b + 1 - core) * 256, 256)
        return remote(wgt.at[:, pl.ds(c, 256)], w_sib.at[b], w_s, w_r.at[g], sib)

    barrier = pltpu.get_barrier_semaphore()
    near_plane = [sib] + [at(x + d, y, core) for d in (1, 3)] + [at(x, y + d, core) for d in (1, 3)]
    near_z = [at_z(lax.rem(z + d, NZ)) for d in (1, NZ - 1)]

    def tell(sem, devices):
        for dev in devices:
            pl.semaphore_signal(sem, inc=1, device_id=dev, device_id_type=MESH)

    tell(barrier, near_plane + near_z)
    tables = [
        pltpu.make_async_copy(tiles_any, tiles, t_sem.at[0]),
        pltpu.make_async_copy(slots_any, slots, t_sem.at[1]),
    ]
    for cp in tables:
        cp.start()
    for q in range(4):
        load_h(q).start()
    for g, group in enumerate(GROUPS):
        for ox, oy in group:
            load_w(blk(ox, oy), g).start()

    pl.semaphore_wait(barrier, 7)

    def hear_plane(k):
        pl.semaphore_wait(ready_p.at[k], 5)

    def hear_z(k):
        pl.semaphore_wait(ready_z.at[k], 2)

    LA, LB = pl.ds(0, CUT), pl.ds(CUT, 640 - CUT)

    def ends(n, p):
        mine_at = pl.ds(z * 8, 8)
        return (
            (slot_out, slot_in.at[z]),
            (down.at[:, p, :, LA], p_da.at[mine_at]),
            (down.at[:, p, :, LB], p_db.at[mine_at]),
            (up.at[:, p], p_up.at[mine_at]),
            (s_da.at[2 * p + core], a_da.at[:, 0, z]),
            (s_db.at[2 * p + core], a_db.at[:, 0, z]),
            (s_up.at[p], a_up.at[:, z]),
        )[n]

    whole = (slot_in, p_da, p_db, p_up, a_da, a_db, a_up)
    others = (
        slot_in.at[pl.ds(0, 7)], p_da.at[pl.ds(0, 56)], p_db.at[pl.ds(0, 56)], p_up.at[pl.ds(0, 56)],
        s_da.at[pl.ds(0, 15)], s_db.at[pl.ds(0, 15)], s_up.at[pl.ds(0, 7)],
    )

    def z_send(n, p):
        src, dst = ends(n, p)
        remote(src, dst, z_s.at[n], z_r.at[n], at_z(p)).start()

    def z_keep(n):
        src, dst = ends(n, z)
        pltpu.make_async_copy(src, dst, z_r.at[n]).start()

    def z_cross(n, p):
        src = (s_da if n == 4 else s_db).at[2 * p + 1 - core]
        dst = (a_da if n == 4 else a_db).at[:, 1, z]
        dev = {"grp": p, "tp": t + 1 - 2 * core}
        remote(src, dst, z_s.at[n], z_r.at[n], dev).start()

    def z_got(n):
        got(whole[n], z_r.at[n])

    def z_sent(n):
        got(others[n], z_s.at[n])

    def ring_z(d):
        return [lax.rem(z + dd, NZ) for dd in ((d, NZ - d) if d < NZ // 2 else (d,))]

    def start1(d, which):
        for n in which:
            for p in ring_z(d):
                z_send(n, p)

    tell(ready_z.at[0], near_z)
    swap_h(0).start()
    swap_w(blk(2, 2), 0).start()
    for q in range(1, 4):
        swap_h(q).start()
    start1(1, (1, 2))
    for g in (1, 2, 3):
        for ox, oy in GROUPS[g]:
            swap_w(blk(ox, oy), g).start()
    tell(ready_p.at[0], near_plane)
    for n in (1, 2, 3):
        z_keep(n)
    for ox, oy in GROUPS[4]:
        swap_w(blk(ox, oy), 4).start()

    far = blk(2, 2)
    got(w_own.at[0], w_l.at[0])
    for f in range(4):
        got(h_own.at[pl.ds(0, 256)], h_l.at[f])
        part[f, 0] = jnp.dot(
            h_own[f * 256:(f + 1) * 256, :], w_own[far], preferred_element_type=F32
        )
    hear_z(0)
    tell(ready_z.at[1], near_z)
    start1(2, (1,))

    def product(q, b):
        r = pl.ds(pl.multiple_of(q * 256, 256), 256)
        return jnp.dot(h_own[r, :], w_own[b], preferred_element_type=F32) + jnp.dot(
            h_sib[r, :], w_sib[b], preferred_element_type=F32
        )

    def order(j):
        return jnp.where(j == 0, 2, jnp.where(j == 1, 1, jnp.where(j == 2, 3, 0)))

    def block_of(f, along, across):
        first = f // 2 == 0
        return blk(jnp.where(first, along, across), jnp.where(first, across, along))

    def ahead(f):
        return jnp.where(lax.rem(f, 2) == 0, 1, 3)

    def other(f):
        return f + 1 - 2 * lax.rem(f, 2)

    def peer1(f):
        first = f // 2 == 0
        d = ahead(f)
        return at(x + jnp.where(first, d, 0), y + jnp.where(first, 0, d), core)

    def peer2(f):
        first = f // 2 == 0
        d = ahead(f)
        return at(x + jnp.where(first, 0, d), y + jnp.where(first, d, 0), core)

    def send_1(f, s, j):
        rsem = s1_r.at[0 if s == 0 else 1, j]
        remote(send1.at[f, s, j], recv1.at[f, s, j], s1_s, rsem, peer1(f)).start()

    def send_2(f, s):
        rsem = s2_r.at[4] if s == 0 else s2_r.at[other(f) if s == 1 else f]
        remote(send2.at[f, s], recv2.at[f, s], s2_s, rsem, peer2(f)).start()

    def need_w(g, n):
        got(w_own.at[pl.ds(0, n)], w_l.at[g])
        got(w_sib.at[pl.ds(0, n)], w_r.at[g])

    got(w_sib.at[0], w_r.at[0])
    for f in range(4):
        got(h_sib.at[pl.ds(0, 256)], h_r.at[f])
        send1[f, 0, 0] = (
            part[f, 0]
            + jnp.dot(h_sib[f * 256:(f + 1) * 256, :], w_sib[far], preferred_element_type=F32)
        ).astype(BF)
        send_1(f, 0, 0)

    def step0(i, _):
        j = i // 4
        f = lax.rem(i, 4)

        @pl.when(f == 0)
        def _():
            need_w(j, 2)

        send1[f, 0, j] = product(f, block_of(f, 2, order(j))).astype(BF)
        send_1(f, 0, j)
        return 0

    hear_z(1)
    tell(ready_z.at[2], near_z)
    for cp in tables:
        cp.wait()
    row = lax.broadcasted_iota(jnp.int32, (8, 128), 0)
    mine = jnp.zeros((8, 128), jnp.int32)
    for i in range(8):
        mine = jnp.where(row == i, slots[tiles[i]], mine)
    slot_out[...] = mine

    z_keep(0)
    start1(3, (1,))
    lax.fori_loop(4, 7, step0, 0)
    hear_z(2)
    for d in (4, 3, 2, 1):
        start1(d, (0,))
    start1(4, (1,))
    start1(2, (2,))
    start1(3, (2,))
    start1(4, (2,))
    lax.fori_loop(7, 16, step0, 0)
    hear_plane(0)
    tell(ready_p.at[1], near_plane)
    need_w(4, 9)

    def near1(i, _):
        j = i // 4
        f = lax.rem(i, 4)
        send1[f, 1, j] = product(other(f), block_of(f, ahead(f), order(j))).astype(BF)
        send_1(f, 1, j)
        return 0

    def near2(i, _):
        j = i // 4
        f = lax.rem(i, 4)
        v = product(f, block_of(f, ahead(f), order(j)))
        @pl.when(f == 0)
        def _():
            got(recv1.at[:, 0, j], s1_r.at[0, j])

        send1[f, 2, j] = (v + recv1[f, 0, j].astype(F32)).astype(BF)
        send_1(f, 2, j)
        return 0

    def step3(i, _):
        j = i // 4
        f = lax.rem(i, 4)
        part[f, j] = product(f, block_of(f, 0, order(j)))
        return 0

    def total1(q, j):
        @pl.when(q == 0)
        def _():
            got(recv1.at[:, pl.ds(1, 2), j], s1_r.at[1, j])

        return part[q, j] + recv1[q, 2, j].astype(F32) + recv1[other(q), 1, j].astype(F32)

    def turn0(q, _):
        send2[q, 0] = total1(q, 0).astype(BF)
        send_2(q, 0)
        return 0

    def turn1(i, _):
        j = 1 + i // 4
        q = lax.rem(i, 4)
        v = total1(q, j)
        keep = lax.rem(q, 2) == j - 1

        @pl.when(keep)
        def _():
            hold[q] = v

        @pl.when(jnp.logical_not(keep))
        def _():
            send2[other(q), 1] = v.astype(BF)
            send_2(other(q), 1)

        return 0

    def turn2(q, _):
        v = hold[q]
        @pl.when(q == 0)
        def _():
            got(recv2.at[:, 0], s2_r.at[4])

        send2[q, 2] = (v + recv2[q, 0].astype(F32)).astype(BF)
        send_2(q, 2)
        return 0

    def turn3(q, _):
        part[q, 3] = total1(q, 3)
        return 0

    def pick(n, src, dst):
        def one(p):
            def body(i, _):
                v = src[slot_s[p, i, 0]]
                if n == 6:
                    dst[p, i] = v
                else:
                    dst[2 * p + lax.rem(i, 2), i // 2] = v
                return 0
            lax.fori_loop(0, 8, body, 0)

        def send(i, _):
            p = lax.rem(z + i, NZ)
            one(p)
            z_send(n, p)
            if n != 6:
                z_cross(n, p)
            return 0

        lax.fori_loop(1, NZ, send, 0)
        one(z)
        z_keep(n)
        if n != 6:
            z_cross(n, z)

    lax.fori_loop(0, 4, near1, 0)
    z_got(0)
    cp = pltpu.make_async_copy(slot_in, slot_s, loc_sem)
    cp.start()
    hear_plane(1)
    tell(ready_p.at[2], near_plane)
    lax.fori_loop(0, 4, near2, 0)
    cp.wait()
    z_got(1)
    pick(4, p_da, s_da)
    lax.fori_loop(4, 8, near1, 0)
    lax.fori_loop(4, 8, near2, 0)
    z_got(2)
    pick(5, p_db, s_db)

    def start_up(i, _):
        z_send(3, lax.rem(z + i, NZ))
        return 0

    lax.fori_loop(1, NZ, start_up, 0)
    lax.fori_loop(8, 12, near1, 0)
    lax.fori_loop(8, 12, near2, 0)
    hear_plane(2)
    tell(ready_p.at[3], near_plane)
    lax.fori_loop(0, 4, step3, 0)
    lax.fori_loop(0, 4, turn0, 0)
    lax.fori_loop(4, 8, step3, 0)
    lax.fori_loop(0, 4, turn1, 0)
    hear_plane(3)
    lax.fori_loop(8, 16, step3, 0)

    def near1_odd(i, _):
        return near1(13 + 2 * i, 0)

    def near1_even(i, _):
        return near1(12 + 2 * i, 0)

    lax.fori_loop(0, 2, near1_odd, 0)

    z_got(4)
    z_got(5)
    nt = (((1,), (1,)), ((), ()))
    for m in range(4):
        r = pl.ds(pl.multiple_of((2 * m + core) * 128, 128), 128)
        v = jnp.zeros((64, 128), F32)
        for k, h in ((0, h_own), (1, h_sib)):
            v += lax.dot_general(
                a_da[m, k].reshape(64, CUT), h[r, 0:CUT], nt, preferred_element_type=F32
            ) + lax.dot_general(
                a_db[m, k].reshape(64, 640 - CUT), h[r, CUT:640], nt, preferred_element_type=F32
            )
        rank_out[pl.ds(m * 4, 4)] = v.astype(BF).reshape(4, 16, 128)

    chip = t // 2

    def send_a(i, _):
        p = lax.rem(chip + i, 16)
        remote(rank_out.at[p], rank_in.at[chip], r_s.at[0], r_r.at[0], at_t(2 * p + core)).start()
        return 0

    def send_b(i, _):
        p = lax.rem(chip + i, 16)
        remote(rank_sum, rank_all.at[0, chip], r_s.at[1], r_r.at[1], at_t(2 * p + core)).start()
        remote(rank_sum, rank_all.at[1, chip], r_s.at[2], r_r.at[2], at_t(2 * p + 1 - core)).start()
        return 0

    lax.fori_loop(1, 16, send_a, 0)
    pltpu.make_async_copy(rank_out.at[chip], rank_in.at[chip], r_r.at[0]).start()
    lax.fori_loop(0, 2, near1_even, 0)
    lax.fori_loop(12, 16, near2, 0)
    z_got(3)
    pick(6, p_up, s_up)
    lax.fori_loop(4, 8, turn1, 0)
    got(rank_in, r_r.at[0])

    def add_rank(i, acc):
        return acc + rank_in[i].astype(F32)

    rank_sum[...] = lax.fori_loop(0, 16, add_rank, jnp.zeros((16, 128), F32)).astype(BF)
    lax.fori_loop(1, 16, send_b, 0)
    pltpu.make_async_copy(rank_sum, rank_all.at[0, chip], r_r.at[1]).start()
    remote(rank_sum, rank_all.at[1, chip], r_s.at[2], r_r.at[2], sib).start()
    lax.fori_loop(0, 4, turn2, 0)

    got(h_sib, h_s)
    got(w_sib, w_s)
    for n in range(6):
        z_sent(n)
    lax.fori_loop(0, 4, turn3, 0)

    got(rank_all.at[0], r_r.at[1])
    z_got(6)

    def adapt(half):
        for m in range(4):
            i = 2 * m + (core if half == 0 else 1 - core)
            v = lax.dot_general(
                rank_all[half, m * 4:m * 4 + 4].reshape(64, 128), a_up[i].reshape(64, 256),
                (((0,), (0,)), ((), ())), preferred_element_type=F32,
            )
            r = pl.ds(pl.multiple_of(lax.rem(i, 2) * 128, 128), 128)
            delta[m, r, :] = (v * adapter_scale).astype(BF).astype(F32)

    adapt(0)
    got(rank_all.at[1], r_r.at[2])
    adapt(1)

    def last(q, _):
        got(recv2.at[q, pl.ds(1, 2)], s2_r.at[q])
        v = part[q, 3] + recv2[q, 2].astype(F32) + recv2[other(q), 1].astype(F32) + delta[q]
        out[pl.ds(pl.multiple_of(q * 256, 256), 256), :] = v.astype(BF)
        return 0

    lax.fori_loop(0, 4, last, 0)
    got(send1, s1_s)
    got(rank_in.at[pl.ds(0, 15)], r_s.at[0])
    got(rank_in.at[pl.ds(0, 15)], r_s.at[1])
    got(rank_all.at[0], r_s.at[2])
    z_sent(6)
    got(send2, s2_s)


def local(hidden, down_weight, adapter_down_factor, adapter_up_factor, row_tile_adapter, adapter_pool_slot):
    any_ = pl.BlockSpec(memory_space=pl.ANY)
    V, D = pltpu.VMEM, pltpu.SemaphoreType.DMA
    down = adapter_down_factor.reshape(8, 8, 8, 640)
    up = adapter_up_factor.reshape(8, 8, 8, 256)
    return pl.pallas_call(
        kernel,
        out_shape=pltpu.VMEM((1024, 256), BF),
        in_specs=[any_] * 6,
        out_specs=pl.BlockSpec(memory_space=pltpu.VMEM),
        scratch_shapes=[
            pltpu.SMEM((8,), jnp.int32), pltpu.SMEM((64,), jnp.int32),
            V((1024, 640), BF), V((1024, 640), BF),
            V((16, 640, 256), BF), V((16, 640, 256), BF),
            V((4, 3, 4, 256, 256), BF), V((4, 3, 4, 256, 256), BF),
            V((4, 3, 256, 256), BF), V((4, 3, 256, 256), BF),
            V((4, 4, 256, 256), F32), V((4, 256, 256), F32),
            V((64, 8, CUT), BF), V((16, 4, 8, CUT), BF), V((4, 2, 8, 8, CUT), BF),
            V((64, 8, 640 - CUT), BF), V((16, 4, 8, 640 - CUT), BF), V((4, 2, 8, 8, 640 - CUT), BF),
            V((64, 8, 256), BF), V((8, 8, 8, 256), BF), V((8, 8, 8, 256), BF),
            V((8, 128), jnp.int32), V((8, 8, 128), jnp.int32), pltpu.SMEM((8, 8, 128), jnp.int32),
            V((16, 16, 128), BF), V((16, 16, 128), BF), V((16, 128), BF), V((2, 16, 16, 128), BF), V((4, 256, 256), F32),
            D((4,)), D, D((4,)), D((5,)), D, D((5,)),
            D, D((2, 4)), D, D((5,)), D((7,)), D((7,)), D((3,)), D((3,)), D, D((2,)),
            pltpu.SemaphoreType.REGULAR((4,)), pltpu.SemaphoreType.REGULAR((3,)),
        ],
        compiler_params=pltpu.CompilerParams(
            collective_id=0, has_side_effects=True, vmem_limit_bytes=60 * 2**20
        ),
    )(hidden, down_weight, down, up, row_tile_adapter, adapter_pool_slot)


def solution(mesh):
    placed = (
        P("grp", "tp"), P("tp", None), P("grp", None, "tp"), P("grp", None, "tp"), P("grp"), P(),
    )
    return jax.shard_map(local, mesh=mesh, in_specs=placed, out_specs=P("grp", "tp"), check_vma=False)
```
